256 devices in a mesh: inl: 64 (over z, y, core), xl: 4 (over x).
Axes of the slice: x: 4, y: 4, z: 8, core: 2. Of those that a mesh axis runs over, the one named last changes fastest.
Arguments:
- traces: float32 [16384, 8, 1024], P(('inl', 'xl')), may hold values from -6 to 6
- owner: int32 [16384, 1], P(('inl', 'xl')), may hold values from 0 to 63; in each aligned block of 64 rows (0 to 63, 64 to 127, ...) at most 2 rows name the same one
- counts: int32 [16384], P(('inl', 'xl')), may hold values from 1 to 8, as said below
- inline_off: int32 [16384, 8], P(('inl', 'xl')), may hold values from 0 to 15
- xline_off: int32 [16384, 8], P(('inl', 'xl')), may hold values from 0 to 63
- phase_cls: int32 [16384, 8], P(('inl', 'xl')), may hold values from 0 to 15
Outputs:
- regular: bfloat16 [1024, 256, 2048], P('inl', 'xl')
The draws below stay inside these ranges and needn't reach their ends.
Inputs may be any that keep to these rules, and one draw needn't show every extreme that they name: Among the blocks of one device, at most 2 name the same owner, a bound that some device reaches. `counts`: blocks whose index is 3 modulo 16 hold a single live trace, blocks whose index is 7 modulo 16 are full, all others hold 6 to 8 live traces.
All inputs are finite; a program needn't handle non-finite values.
Results may differ from the reference program's by a relative error of at most 0.0042.
Values sent between devices are 32-bit elements; how exact they have to be, the bound alone decides.
A program may use at most 64 MiB of HBM per device.

```python
import math
import jax
import jax.numpy as jnp
import numpy as np

SAMPLES = 1024
XLINES = 256
TAPS = 8
PHASES = 16
BLOCK_TR = 8
SLOTS = 2
IL_DEV = 16
XL_DEV = 64
INLINES = 1024
BLOCKS_DEV = 64
BLOCKS = 16384
N_INL = 64
N_XL = 4


def draw_counts(key, part):
    drawn = jax.random.randint(jax.random.fold_in(key, 11), (BLOCKS,), 6, BLOCK_TR + 1, dtype=jnp.int32)
    position = jnp.arange(BLOCKS, dtype=jnp.int32) % 16
    drawn = jnp.where(position == 3, jnp.int32(1), drawn)
    drawn = jnp.where(position == 7, jnp.int32(BLOCK_TR), drawn)
    return drawn


def set_ends(values, rng, smallest, high):
    index_at = [jax.random.randint(jax.random.fold_in(rng, axis), (), 0, length) for axis, length in enumerate(values.shape)]
    widest = values.shape.index(max(values.shape))
    neighbour = index_at[:widest] + [(index_at[widest] + 1) % values.shape[widest]] + index_at[widest + 1:]
    return values.at[tuple(index_at)].set(smallest).at[tuple(neighbour)].set(high)


def steps_of(rng, shape, split, least, top_value):
    level = 1.0
    for dim, parts in split:
        draws = jax.random.uniform(jax.random.fold_in(jax.random.fold_in(rng, 6), dim), (parts,), jnp.float32, least / len(split), top_value / len(split))
        level = level * jnp.repeat(jnp.exp(draws), shape[dim] // parts).reshape((-1,) + (1,) * (len(shape) - 1 - dim))
    return level


def deal_out(rng, own, number, rows, amount, top, bound, slope):
    ranking = jax.random.permutation(rng, amount)
    crowded, usual = shares(amount, rows * top, bound, slope, True), shares(amount, rows * top, bound, slope, False)
    places = jnp.arange(amount)

    def named(sizes, rotation):
        used = int((sizes > 0).sum())
        fixed = max(1, used // 4)
        passed = fixed + (places - fixed + rotation * (used - fixed)) % max(1, amount - fixed)
        return jnp.zeros((amount,), jnp.int32).at[ranking[jnp.where(places < fixed, places, passed)]].set(jnp.asarray(sizes, jnp.int32))

    sizes = jnp.where(number % 4 == 0, named(crowded, number // 4), named(usual, number - number // 4 - 1))
    mixed = jax.random.permutation(jax.random.fold_in(own, 3), amount)
    source_of, receiver = mixed[0:amount // 2 * 2:2], mixed[1:amount // 2 * 2:2]
    margin = jnp.minimum(sizes[source_of] - 1, bound - sizes[receiver]) // 2
    margin = jnp.where((source_of == ranking[0]) | (receiver == ranking[0]) | (sizes[receiver] == 0), 0, jnp.maximum(margin, 0))
    passed = jax.random.randint(jax.random.fold_in(own, 4), (amount // 2,), 0, 1 << 20) % (margin + 1)
    sizes = sizes.at[source_of].add(-passed).at[receiver].add(passed)
    labels = jnp.searchsorted(jnp.cumsum(sizes), jnp.arange(rows * top), side="right").astype(jnp.int32)
    table = labels.reshape(top, rows).T
    table = table[jax.random.permutation(jax.random.fold_in(own, 1), rows)]
    rotation = jax.random.randint(jax.random.fold_in(own, 2), (rows, 1), 0, top)
    return jnp.take_along_axis(table, (jnp.arange(top)[None, :] + rotation) % top, axis=1)


def shares(count, total, reach, skew, full):
    weights = [(1 << 20) // math.isqrt(standing ** skew) + 1 for standing in range(1, count + 1)]
    largest = reach if full else min(reach, max(-(-total // count), total * weights[0] // sum(weights)))
    least = 1 if total - largest >= count - 1 else 0
    given, surplus = [largest] + [least] * (count - 1), total - largest - least * (count - 1)
    while surplus > 0:
        candidates = [i for i in range(1, count) if given[i] < largest] or [i for i in range(1, count) if given[i] < reach]
        pool, budget = sum([weights[i] for i in candidates]), surplus
        for i in candidates:
            more = min(reach - given[i], max(1, budget * weights[i] // pool), surplus)
            given[i] = given[i] + more
            surplus = surplus - more
    return np.array(given)


def scatter_about(own_key, dims, spread, limit, shards=(), held_as=jnp.bfloat16):
    gain = steps_of(own_key, dims, shards, -0.22, 0.18) if shards else 1.0
    entries = jax.random.normal(own_key, dims, jnp.float32) * spread * gain
    return jnp.minimum(jnp.maximum(entries, -limit), limit).astype(held_as)


def setup_inputs(seed: int = 0) -> dict:
    streams_of = jax.random.split(jax.random.key(seed), 7)
    traces = scatter_about(streams_of[0], (BLOCKS, BLOCK_TR, SAMPLES), 1.0, 6.0, ((0, 256),), jnp.float32)
    owner_keys = jax.random.split(jax.random.fold_in(streams_of[1], 1), BLOCKS // BLOCKS_DEV)
    owner_turns = jax.random.permutation(jax.random.fold_in(streams_of[1], 3), BLOCKS // BLOCKS_DEV)
    owner = jax.vmap(lambda own, number: deal_out(jax.random.fold_in(streams_of[1], 2), own, number, BLOCKS_DEV, N_INL, 1, SLOTS, 2))(owner_keys, owner_turns).reshape((BLOCKS, 1))
    counts = draw_counts(jax.random.fold_in(streams_of[6], 71), 0)
    inline_off = set_ends(jax.random.randint(streams_of[3], (BLOCKS, BLOCK_TR), 0, IL_DEV), jax.random.fold_in(streams_of[3], 1), 0, IL_DEV - 1).astype(jnp.int32)
    xline_off = set_ends(jax.random.randint(streams_of[4], (BLOCKS, BLOCK_TR), 0, XL_DEV), jax.random.fold_in(streams_of[4], 1), 0, XL_DEV - 1).astype(jnp.int32)
    phase_cls = set_ends(jax.random.randint(streams_of[5], (BLOCKS, BLOCK_TR), 0, PHASES), jax.random.fold_in(streams_of[5], 1), 0, PHASES - 1).astype(jnp.int32)
    return dict(traces=traces, owner=owner, counts=counts, inline_off=inline_off, xline_off=xline_off, phase_cls=phase_cls)


def sinc_table():
    phase_idx = jnp.arange(PHASES, dtype=jnp.int32).astype(jnp.float32)[:, None]
    tap_idx = jnp.arange(TAPS, dtype=jnp.int32).astype(jnp.float32)[None, :]
    offset = tap_idx - 3.0 - phase_idx / PHASES
    return jnp.sinc(offset) * (0.5 + 0.5 * jnp.cos(math.pi * offset / 4.0))


def resample_table(length):
    rows_idx = jnp.arange(length, dtype=jnp.int32)[:, None]
    cols_idx = jnp.arange(2 * length, dtype=jnp.int32)[None, :]
    lagged = cols_idx // 2 - rows_idx
    parity = cols_idx % 2
    sign_val = (1 - 2 * (lagged % 2)).astype(jnp.float32)
    odd_val = sign_val / (math.pi * (lagged.astype(jnp.float32) + 0.5))
    even_val = (lagged == 0).astype(jnp.float32)
    return jnp.where(parity == 1, odd_val, even_val).astype(jnp.bfloat16)


def reference(traces, owner, counts, inline_off, xline_off, phase_cls):
    blocks_all = traces.shape[0]
    device_idx = jnp.arange(blocks_all, dtype=jnp.int32) // BLOCKS_DEV
    band_idx = device_idx % N_XL
    target_inl = owner[:, 0][:, None] * IL_DEV + inline_off
    target_xl = (band_idx * XL_DEV)[:, None] + xline_off
    live = (jnp.arange(BLOCK_TR, dtype=jnp.int32)[None, :] < counts[:, None]).astype(jnp.float32)
    weights = sinc_table()[phase_cls] * live[:, :, None]
    stack = jnp.zeros((INLINES, XLINES + TAPS - 1, SAMPLES), jnp.float32)
    fold = jnp.zeros((INLINES, XLINES + TAPS - 1), jnp.float32)
    for tap in range(TAPS):
        stack = stack.at[target_inl, target_xl + tap].add(weights[:, :, tap, None] * traces)
        fold = fold.at[target_inl, target_xl + tap].add(weights[:, :, tap])
    stack = stack[:, 3:3 + XLINES]
    fold = fold[:, 3:3 + XLINES]
    binned = (stack / jnp.maximum(fold, 0.25)[:, :, None]).astype(jnp.bfloat16)
    flat_out = jnp.dot(binned.reshape(INLINES * XLINES, SAMPLES), resample_table(SAMPLES), preferred_element_type=jnp.float32)
    return flat_out.reshape(INLINES, XLINES, 2 * SAMPLES).astype(jnp.bfloat16)
```

```python
import functools
import math

import jax
import jax.numpy as jnp
from jax import lax
from jax.experimental import pallas as pl
from jax.experimental.pallas import tpu as pltpu
from jax.sharding import PartitionSpec as P

XLINES = 256
TAPS = 8
PHASES = 16
BLOCK_TR = 8
SLOTS = 2
IL_DEV = 16
CHUNKS = 4
CAP = 3
LANES = 128
ROWS = SLOTS * BLOCK_TR
MESH = pl.DeviceIdType.MESH


def sinc_table():
    phase_idx = jnp.arange(PHASES, dtype=jnp.int32).astype(jnp.float32)[:, None]
    tap_idx = jnp.arange(TAPS, dtype=jnp.int32).astype(jnp.float32)[None, :]
    offset = tap_idx - 3.0 - phase_idx / PHASES
    return jnp.sinc(offset) * (0.5 + 0.5 * jnp.cos(math.pi * offset / 4.0))


def wait_for(ref, sem):
    pltpu.make_async_copy(ref, ref, sem).wait()


def build_resample(table_ref):
    length, width = table_ref.shape
    step = 16

    def body(part, carry):
        base = pl.multiple_of(part * step, step)
        rows_idx = lax.broadcasted_iota(jnp.int32, (step, width), 0) + base
        cols_idx = lax.broadcasted_iota(jnp.int32, (step, width), 1)
        lagged = (cols_idx >> 1) - rows_idx
        sign_val = (1 - 2 * (lagged & 1)).astype(jnp.float32)
        odd_val = sign_val / (math.pi * (lagged.astype(jnp.float32) + 0.5))
        even_val = (lagged == 0).astype(jnp.float32)
        table_ref[pl.ds(base, step), :] = jnp.where((cols_idx & 1) == 1, odd_val, even_val).astype(
            jnp.bfloat16
        )
        return carry

    lax.fori_loop(0, length // step, body, 0)


def padded_kernel(
    n_inl,
    n_xl,
    index_ref,
    traces_hbm,
    nav_ref,
    taps_ref,
    out_hbm,
    traces,
    send,
    recv,
    nav_send,
    nav_recv,
    inner,
    outer_f32,
    outer,
    resample,
    total,
    stack,
    out_rows,
    halo_send,
    halo_recv,
    fold_in,
    fold_send,
    fold_recv,
    load_sem,
    send_sems,
    recv_sems,
    nav_send_sem,
    nav_recv_sem,
    halo_send_sems,
    halo_recv_sems,
    fold_send_sems,
    fold_recv_sems,
    out_sem,
):
    me = lax.axis_index("inl")
    band = lax.axis_index("xl")
    right, left = lax.rem(band + 1, n_xl), lax.rem(band + n_xl - 1, n_xl)
    chunk = traces.shape[2] // CHUNKS
    depth = n_inl * ROWS
    width = inner.shape[0] // IL_DEV
    padded = width + 2 * TAPS
    side = IL_DEV * TAPS

    load = pltpu.make_async_copy(traces_hbm, traces, load_sem)
    load.start()

    barrier = pltpu.get_barrier_semaphore()

    def greet(off, carry):
        dest = lax.rem(me + off, n_inl)
        pl.semaphore_signal(barrier, inc=1, device_id={"inl": dest}, device_id_type=MESH)
        return carry

    lax.fori_loop(1, n_inl, greet, 0)
    for neighbour in (left, right):
        pl.semaphore_signal(barrier, inc=1, device_id={"xl": neighbour}, device_id_type=MESH)

    def gather_nav(off, carry):
        dest = lax.rem(me + off, n_inl)
        for slot in range(SLOTS):
            block = index_ref[dest, slot]
            nav_send[dest, slot * BLOCK_TR : (slot + 1) * BLOCK_TR, :] = nav_ref[block]
        return carry

    lax.fori_loop(0, n_inl, gather_nav, 0)
    nav_recv[me] = nav_send[me]
    load.wait()

    def gather(c):
        def body(off, carry):
            dest = lax.rem(me + off, n_inl)
            for slot in range(SLOTS):
                block = index_ref[dest, SLOTS + slot]
                send[c, dest, slot * BLOCK_TR : (slot + 1) * BLOCK_TR, :] = traces[
                    block, :, c * chunk : (c + 1) * chunk
                ]
            return carry

        lax.fori_loop(0, n_inl, body, 0)
        recv[c, me] = send[c, me]

    gather(0)
    pl.semaphore_wait(barrier, n_inl - 1 + 2)

    def push_nav(off, carry):
        dest = lax.rem(me + off, n_inl)
        pltpu.make_async_remote_copy(
            src_ref=nav_send.at[dest],
            dst_ref=nav_recv.at[me],
            send_sem=nav_send_sem,
            recv_sem=nav_recv_sem,
            device_id={"inl": dest},
            device_id_type=MESH,
        ).start()
        return carry

    lax.fori_loop(1, n_inl, push_nav, 0)

    def push(c):
        def body(off, carry):
            dest = lax.rem(me + off, n_inl)
            pltpu.make_async_remote_copy(
                src_ref=send.at[c, dest],
                dst_ref=recv.at[c, me],
                send_sem=send_sems.at[c],
                recv_sem=recv_sems.at[c],
                device_id={"inl": dest},
                device_id_type=MESH,
            ).start()
            return carry

        lax.fori_loop(1, n_inl, body, 0)

    for c in range(CHUNKS):
        if c + 1 < CHUNKS:
            gather(c + 1)
        push(c)

    build_resample(resample)

    wait_for(nav_recv.at[pl.ds(0, n_inl - 1)], nav_recv_sem)
    nav = nav_recv[...].reshape(depth, LANES).T
    inl_ids, xl_ids, cls_ids, live = nav[0:1], nav[1:2], nav[2:3], nav[3:4]
    weights = jnp.zeros((TAPS, depth), jnp.float32)
    for phase in range(PHASES):
        weights = jnp.where(cls_ids == float(phase), taps_ref[:, phase : phase + 1], weights)
    weights = weights * live
    tap_of = lax.broadcasted_iota(jnp.int32, (padded, depth), 0).astype(jnp.float32) - (xl_ids + 5.0)
    spread = jnp.zeros((padded, depth), jnp.float32)
    for tap in range(TAPS):
        spread = jnp.where(tap_of == float(tap), weights[tap : tap + 1], spread)

    def line(i, carry):
        rows = jnp.where(inl_ids == i.astype(jnp.float32), spread, 0.0)
        sums = jnp.broadcast_to(jnp.sum(rows, axis=1, keepdims=True), (padded, LANES))
        base = pl.multiple_of(i * width, width)
        inner[pl.ds(base, width), :] = rows[TAPS : TAPS + width].astype(jnp.bfloat16)
        fold_in[pl.ds(base, width), :] = sums[TAPS : TAPS + width]
        edge = pl.multiple_of(i * TAPS, TAPS)
        outer_f32[0, pl.ds(edge, TAPS), :] = rows[:TAPS]
        outer_f32[1, pl.ds(edge, TAPS), :] = rows[TAPS + width :]
        fold_send[0, pl.ds(edge, TAPS), :] = sums[:TAPS]
        fold_send[1, pl.ds(edge, TAPS), :] = sums[TAPS + width :]
        return carry

    lax.fori_loop(0, IL_DEV, line, 0)
    outer[...] = outer_f32[...].astype(jnp.bfloat16).reshape(2 * side, depth)

    folds = []
    for way, neighbour in ((0, left), (1, right)):
        copy = pltpu.make_async_remote_copy(
            src_ref=fold_send.at[way],
            dst_ref=fold_recv.at[way],
            send_sem=fold_send_sems.at[way],
            recv_sem=fold_recv_sems.at[way],
            device_id={"xl": neighbour},
            device_id_type=MESH,
        )
        copy.start()
        folds.append(copy)

    from_right = jnp.where(band < n_xl - 1, 1.0, 0.0)
    from_left = jnp.where(band > 0, 1.0, 0.0)

    for copy in folds:
        copy.wait()

    def join(i, carry):
        edge = pl.multiple_of(i * TAPS, TAPS)
        first = pl.multiple_of(i * width, TAPS)
        last = pl.multiple_of(i * width + width - TAPS, TAPS)
        fold_in[pl.ds(last, TAPS), :] += fold_recv[0, pl.ds(edge, TAPS), :] * from_right
        fold_in[pl.ds(first, TAPS), :] += fold_recv[1, pl.ds(edge, TAPS), :] * from_left
        return carry

    lax.fori_loop(0, IL_DEV, join, 0)
    fold_in[...] = 1.0 / jnp.maximum(fold_in[...], 0.25)

    halos = []
    for c in range(CHUNKS):
        wait_for(recv.at[c, pl.ds(0, n_inl - 1)], recv_sems.at[c])
        block = recv[c].reshape(depth, chunk).astype(jnp.bfloat16)
        halo_send[c] = jnp.dot(outer[...], block, preferred_element_type=jnp.float32).reshape(
            2, side, chunk
        )
        stack[...] = jnp.dot(inner[...], block, preferred_element_type=jnp.float32)
        sent = []
        for way, neighbour in ((0, left), (1, right)):
            copy = pltpu.make_async_remote_copy(
                src_ref=halo_send.at[c, way],
                dst_ref=halo_recv.at[c, way],
                send_sem=halo_send_sems.at[c, way],
                recv_sem=halo_recv_sems.at[c, way],
                device_id={"xl": neighbour},
                device_id_type=MESH,
            )
            copy.start()
            sent.append(copy)
        for copy in sent:
            copy.wait()

        def add_halo(i, carry, c=c):
            edge = pl.multiple_of(i * TAPS, TAPS)
            first = pl.multiple_of(i * width, TAPS)
            last = pl.multiple_of(i * width + width - TAPS, TAPS)
            stack[pl.ds(last, TAPS), :] += halo_recv[c, 0, pl.ds(edge, TAPS), :] * from_right
            stack[pl.ds(first, TAPS), :] += halo_recv[c, 1, pl.ds(edge, TAPS), :] * from_left
            return carry

        lax.fori_loop(0, IL_DEV, add_halo, 0)

        tile = out_rows.shape[0] // TAPS

        def finish(m, carry, c=c):
            base = pl.multiple_of(m * tile, tile)
            scale = fold_in[pl.ds(base, tile), 0:1]
            binned = (stack[pl.ds(base, tile), :] * scale).astype(jnp.bfloat16)
            part = jnp.dot(
                binned, resample[c * chunk : (c + 1) * chunk, :], preferred_element_type=jnp.float32
            )
            if c > 0:
                part = part + total[pl.ds(base, tile), :]
            if c < CHUNKS - 1:
                total[pl.ds(base, tile), :] = part
            else:
                out_rows[pl.ds(base, tile), :] = part.astype(jnp.bfloat16)
                pltpu.make_async_copy(
                    out_rows.at[pl.ds(base, tile)], out_hbm.at[pl.ds(base, tile)], out_sem
                ).start()
            return carry

        lax.fori_loop(0, TAPS, finish, 0)

    wait_for(nav_send.at[pl.ds(0, n_inl - 1)], nav_send_sem)
    for c in range(CHUNKS):
        wait_for(send.at[c, pl.ds(0, n_inl - 1)], send_sems.at[c])
    wait_for(out_rows, out_sem)


def padded_plan(traces, owner, counts, inline_off, xline_off, phase_cls):
    n_inl, n_xl = lax.axis_size("inl"), lax.axis_size("xl")
    local_blocks, _, samples = traces.shape
    width = XLINES // n_xl
    chunk = samples // CHUNKS
    depth = n_inl * ROWS
    side = IL_DEV * TAPS
    block_idx = jnp.arange(local_blocks, dtype=jnp.int32)
    named = owner[:, 0][None, :] == jnp.arange(n_inl, dtype=jnp.int32)[:, None]
    low = jnp.min(jnp.where(named, block_idx[None, :], local_blocks), axis=1)
    high = jnp.max(jnp.where(named, block_idx[None, :], -1), axis=1)
    high = jnp.where(high > low, high, local_blocks)
    nav_index = jnp.stack([low, high], axis=1)
    index = jnp.concatenate([nav_index, jnp.minimum(nav_index, local_blocks - 1)], axis=1)
    live = (jnp.arange(BLOCK_TR, dtype=jnp.int32)[None, :] < counts[:, None]).astype(jnp.float32)
    parts = [inline_off.astype(jnp.float32), xline_off.astype(jnp.float32)]
    parts = parts + [phase_cls.astype(jnp.float32), live]
    nav = jnp.stack(parts, axis=2)
    nav = jnp.pad(nav, ((0, 1), (0, 0), (0, LANES - len(parts))))
    taps = sinc_table().T
    scratch = [
        pltpu.VMEM((local_blocks, BLOCK_TR, samples), jnp.float32),
        pltpu.VMEM((CHUNKS, n_inl, ROWS, chunk), jnp.float32),
        pltpu.VMEM((CHUNKS, n_inl, ROWS, chunk), jnp.float32),
        pltpu.VMEM((n_inl, ROWS, LANES), jnp.float32),
        pltpu.VMEM((n_inl, ROWS, LANES), jnp.float32),
        pltpu.VMEM((IL_DEV * width, depth), jnp.bfloat16),
        pltpu.VMEM((2, side, depth), jnp.float32),
        pltpu.VMEM((2 * side, depth), jnp.bfloat16),
        pltpu.VMEM((samples, 2 * samples), jnp.bfloat16),
        pltpu.VMEM((IL_DEV * width, 2 * samples), jnp.float32),
        pltpu.VMEM((IL_DEV * width, chunk), jnp.float32),
        pltpu.VMEM((IL_DEV * width, 2 * samples), jnp.bfloat16),
        pltpu.VMEM((CHUNKS, 2, side, chunk), jnp.float32),
        pltpu.VMEM((CHUNKS, 2, side, chunk), jnp.float32),
        pltpu.VMEM((IL_DEV * width, LANES), jnp.float32),
        pltpu.VMEM((2, side, LANES), jnp.float32),
        pltpu.VMEM((2, side, LANES), jnp.float32),
        pltpu.SemaphoreType.DMA,
        pltpu.SemaphoreType.DMA((CHUNKS,)),
        pltpu.SemaphoreType.DMA((CHUNKS,)),
        pltpu.SemaphoreType.DMA,
        pltpu.SemaphoreType.DMA,
        pltpu.SemaphoreType.DMA((CHUNKS, 2)),
        pltpu.SemaphoreType.DMA((CHUNKS, 2)),
        pltpu.SemaphoreType.DMA((2,)),
        pltpu.SemaphoreType.DMA((2,)),
        pltpu.SemaphoreType.DMA,
    ]
    out = pl.pallas_call(
        functools.partial(padded_kernel, n_inl, n_xl),
        out_shape=jax.ShapeDtypeStruct((IL_DEV * width, 2 * samples), jnp.bfloat16),
        in_specs=[
            pl.BlockSpec(memory_space=pltpu.SMEM),
            pl.BlockSpec(memory_space=pl.ANY),
            pl.BlockSpec(memory_space=pltpu.VMEM),
            pl.BlockSpec(memory_space=pltpu.VMEM),
        ],
        out_specs=pl.BlockSpec(memory_space=pl.ANY),
        scratch_shapes=scratch,
        compiler_params=pltpu.CompilerParams(
            collective_id=1, has_side_effects=True, vmem_limit_bytes=44 << 20
        ),
    )(index, traces, nav, taps)
    return out.reshape(IL_DEV, width, 2 * samples)


EDGES = (0, 3, 5, 7, 8)
PARTS = len(EDGES) - 1


def span_of(c, length):
    return EDGES[c] * length // EDGES[-1], EDGES[c + 1] * length // EDGES[-1]


def widest(length):
    return max(hi - lo for lo, hi in [span_of(c, length) for c in range(PARTS)])


def plane_of(n_inl):
    return 8 if n_inl % 8 == 0 and n_inl > 8 else 2


def plan_kernel(n_inl, owner_ref, counts_ref, inl_ref, xl_ref, cls_ref, table_ref, nav_ref, taps_ref):
    blocks = owner_ref.shape[1]
    plane = plane_of(n_inl)
    named = owner_ref[...] == lax.broadcasted_iota(jnp.int32, (n_inl, blocks), 0)
    block_idx = lax.broadcasted_iota(jnp.int32, (n_inl, blocks), 1).astype(jnp.float32)
    low = jnp.min(jnp.where(named, block_idx, float(blocks)), axis=1, keepdims=True)
    high = jnp.max(jnp.where(named, block_idx, -1.0), axis=1, keepdims=True)
    two = jnp.broadcast_to(jnp.where(high > low, 1.0, 0.0), (n_inl, LANES))
    row_id = lax.broadcasted_iota(jnp.int32, (n_inl, n_inl), 0)
    col_id = lax.broadcasted_iota(jnp.int32, (n_inl, n_inl), 1)
    ahead = jnp.where((col_id < row_id) & (col_id // plane == row_id // plane), 1.0, 0.0)
    rank = jnp.dot(ahead, two, preferred_element_type=jnp.float32)
    own = lax.broadcasted_iota(jnp.int32, (n_inl, LANES), 0)
    lane = lax.broadcasted_iota(jnp.int32, (n_inl, LANES), 1)
    slot = (own // plane * CAP).astype(jnp.float32) + rank
    chosen = (two > 0.5) & (rank < CAP - 0.5) & (slot == lane.astype(jnp.float32))
    taken = jnp.sum(jnp.where(chosen, 1.0, 0.0), axis=0, keepdims=True)
    second = jnp.sum(jnp.where(chosen, high, 0.0), axis=0, keepdims=True)
    second = jnp.where(taken > 0.5, second, float(blocks))
    target = jnp.where(chosen, (own % plane + 1).astype(jnp.float32), 0.0)
    target = jnp.sum(target, axis=0, keepdims=True)
    over = jnp.where((two > 0.5) & (rank > CAP - 0.5), 1.0, 0.0)
    over = jnp.max(over, axis=0, keepdims=True)
    table_ref[:n_inl, :] = jnp.broadcast_to(low, (n_inl, LANES)).astype(jnp.int32)
    table_ref[n_inl : n_inl + 1, :] = second.astype(jnp.int32)
    table_ref[n_inl + 1 : n_inl + 2, :] = target.astype(jnp.int32)
    table_ref[n_inl + 2 : n_inl + 3, :] = over.astype(jnp.int32)
    table_ref[n_inl + 3 :, :] = jnp.zeros((5, LANES), jnp.int32)
    tap = lax.broadcasted_iota(jnp.int32, (TAPS, LANES), 0).astype(jnp.float32)
    offset = tap - 3.0 - lax.broadcasted_iota(jnp.int32, (TAPS, LANES), 1).astype(jnp.float32) / PHASES
    at_zero = offset == 0.0
    angle = math.pi * jnp.where(at_zero, 1.0, offset)
    sinc = jnp.where(at_zero, 1.0, jnp.sin(angle) / angle)
    taps_ref[...] = sinc * (0.5 + 0.5 * jnp.cos(math.pi * offset / 4.0))
    trace_idx = lax.broadcasted_iota(jnp.int32, (BLOCK_TR, blocks), 0)
    fields = [inl_ref[...], xl_ref[...], cls_ref[...], (trace_idx < counts_ref[...]).astype(jnp.int32)]
    fields = [field.astype(jnp.float32) for field in fields]
    field_id = lax.broadcasted_iota(jnp.int32, (BLOCK_TR, LANES), 1)
    for block in range(blocks):
        tile = jnp.zeros((BLOCK_TR, LANES), jnp.float32)
        for place, field in enumerate(fields):
            tile = jnp.where(field_id == place, field[:, block : block + 1], tile)
        nav_ref[block] = tile
    nav_ref[blocks] = jnp.zeros((BLOCK_TR, LANES), jnp.float32)


def fast_kernel(
    n_inl,
    n_xl,
    table_ref,
    traces_hbm,
    nav_ref,
    taps_ref,
    total,
    tail_ref,
    binned_ref,
    flag_ref,
    traces,
    p_send,
    p_recv,
    z_send,
    z_recv,
    y_send,
    y_recv,
    p_nav_send,
    p_nav_recv,
    z_nav_send,
    z_nav_recv,
    y_nav_send,
    y_nav_recv,
    samples_in,
    inner,
    outer_f32,
    outer,
    resample,
    stack,
    halo_send,
    halo_recv,
    fold_in,
    fold_send,
    fold_recv,
    flag_send,
    flag_recv,
    load_sem,
    p_sems,
    z_sems,
    y_sems,
    nav_sems,
    halo_sems,
    fold_sems,
    flag_sems,
):
    me = lax.axis_index("inl")
    band = lax.axis_index("xl")
    plane = plane_of(n_inl)
    layers = n_inl // plane
    layer, place = me // plane, lax.rem(me, plane)
    right, left = lax.rem(band + 1, n_xl), lax.rem(band + n_xl - 1, n_xl)
    length = traces.shape[2]
    blocks = traces.shape[0]
    half = n_inl * BLOCK_TR
    depth = 2 * half
    width = inner.shape[0] // IL_DEV
    padded = width + 2 * TAPS
    side = IL_DEV * TAPS

    load = pltpu.make_async_copy(traces_hbm, traces, load_sem)
    load.start()

    barrier = pltpu.get_barrier_semaphore()

    def greet(off, carry):
        dest = lax.rem(me + 1 + lax.rem(off + n_inl * 7 // 16, n_inl - 1), n_inl)
        pl.semaphore_signal(barrier, inc=1, device_id={"inl": dest}, device_id_type=MESH)
        return carry

    lax.fori_loop(0, n_inl - 1, greet, 0)
    for step in range(1, n_xl):
        other = lax.rem(band + step, n_xl)
        pl.semaphore_signal(barrier, inc=1, device_id={"xl": other}, device_id_type=MESH)

    field_id = lax.broadcasted_iota(jnp.int32, (BLOCK_TR, LANES), 1)
    over = table_ref[n_inl + 2, 0].astype(jnp.float32)
    load.wait()

    def gather_second(layer_to, carry):
        for r in range(CAP):
            spot = layer_to * CAP + r
            block = table_ref[n_inl, spot]
            target = table_ref[n_inl + 1, spot].astype(jnp.float32)
            z_nav_send[layer_to, r] = jnp.where(field_id == 4, target, nav_ref[block])
            z_send[layer_to, r * BLOCK_TR : (r + 1) * BLOCK_TR, :] = traces[
                jnp.minimum(block, blocks - 1)
            ]
        return carry

    lax.fori_loop(0, layers, gather_second, 0)

    def gather_first(off, carry):
        dest = lax.rem(me + off, n_inl)
        block = table_ref[dest, 0]
        p_nav_send[dest] = jnp.where(field_id == 5, over, nav_ref[block])
        p_send[dest] = traces[jnp.minimum(block, blocks - 1)]
        return carry

    lax.fori_loop(0, n_inl, gather_first, 0)
    p_nav_recv[me] = p_nav_send[me]
    p_recv[me] = p_send[me]
    z_nav_recv[layer] = z_nav_send[layer]
    z_recv[layer] = z_send[layer]

    pl.semaphore_wait(barrier, n_inl - 1 + n_xl - 1)

    def span(c):
        lo, hi = span_of(c, length)
        return pl.ds(lo, hi - lo)

    def push(source, target, sems, to):
        pltpu.make_async_remote_copy(
            src_ref=source,
            dst_ref=target,
            send_sem=sems[0],
            recv_sem=sems[1],
            device_id=to,
            device_id_type=MESH,
        ).start()

    def push_first(c):
        def body(off, carry):
            dest = lax.rem(me + off, n_inl)
            push(
                p_send.at[dest, :, span(c)],
                p_recv.at[me, :, span(c)],
                (p_sems.at[0, c], p_sems.at[1, c]),
                {"inl": dest},
            )
            return carry

        lax.fori_loop(1, n_inl, body, 0)

    def push_second(c):
        def body(off, carry):
            to = lax.rem(layer + off, layers)
            push(
                z_send.at[to, :, span(c)],
                z_recv.at[layer, :, span(c)],
                (z_sems.at[0, c], z_sems.at[1, c]),
                {"inl": to * plane + place},
            )
            return carry

        lax.fori_loop(1, layers, body, 0)

    def spread_second(c):
        lo, hi = span_of(c, length)
        wait_for(z_recv.at[pl.ds(0, layers - 1), :, span(c)], z_sems.at[1, c])

        def body(to, carry):
            wanted = (to + 1).astype(jnp.float32)
            for origin in range(layers):
                held = jnp.zeros((BLOCK_TR, hi - lo), jnp.float32)
                for r in range(CAP):
                    named = z_nav_recv[origin, r, :, 4:5] == wanted
                    value = z_recv[origin, r * BLOCK_TR : (r + 1) * BLOCK_TR, lo:hi]
                    held = jnp.where(named, value, held)
                y_send[to, origin * BLOCK_TR : (origin + 1) * BLOCK_TR, lo:hi] = held
            return carry

        lax.fori_loop(0, plane, body, 0)
        y_recv[place, :, lo:hi] = y_send[place, :, lo:hi]

        def send(off, carry):
            to = lax.rem(place + off, plane)
            push(
                y_send.at[to, :, span(c)],
                y_recv.at[place, :, span(c)],
                (y_sems.at[0, c], y_sems.at[1, c]),
                {"inl": layer * plane + to},
            )
            return carry

        lax.fori_loop(1, plane, send, 0)

    def push_z_nav(off, carry):
        to = lax.rem(layer + off, layers)
        push(
            z_nav_send.at[to],
            z_nav_recv.at[layer],
            (nav_sems.at[0, 1], nav_sems.at[1, 1]),
            {"inl": to * plane + place},
        )
        return carry

    def push_p_nav(off, carry):
        dest = lax.rem(me + off, n_inl)
        push(
            p_nav_send.at[dest],
            p_nav_recv.at[me],
            (nav_sems.at[0, 0], nav_sems.at[1, 0]),
            {"inl": dest},
        )
        return carry

    push_second(0)
    lax.fori_loop(1, layers, push_z_nav, 0)
    push_second(1)
    push_first(0)
    lax.fori_loop(1, n_inl, push_p_nav, 0)
    push_second(2)
    push_first(1)

    wait_for(z_nav_recv.at[pl.ds(0, layers - 1)], nav_sems.at[1, 1])

    def spread_nav(to, carry):
        wanted = (to + 1).astype(jnp.float32)
        for origin in range(layers):
            held = jnp.zeros((BLOCK_TR, LANES), jnp.float32)
            for r in range(CAP):
                tile = z_nav_recv[origin, r]
                held = jnp.where(tile[:, 4:5] == wanted, tile, held)
            y_nav_send[to, origin] = held
        return carry

    lax.fori_loop(0, plane, spread_nav, 0)
    y_nav_recv[place] = y_nav_send[place]

    def push_y_nav(off, carry):
        to = lax.rem(place + off, plane)
        push(
            y_nav_send.at[to],
            y_nav_recv.at[place],
            (nav_sems.at[0, 2], nav_sems.at[1, 2]),
            {"inl": layer * plane + to},
        )
        return carry

    lax.fori_loop(1, plane, push_y_nav, 0)
    spread_second(0)
    build_resample(resample)
    tail_ref[...] = resample[span_of(PARTS - 1, length)[0] :, :]
    spread_second(1)
    push_second(3)
    push_first(2)

    wait_for(p_nav_recv.at[pl.ds(0, n_inl - 1)], nav_sems.at[1, 0])
    wait_for(y_nav_recv.at[pl.ds(0, plane - 1)], nav_sems.at[1, 2])
    first_nav = p_nav_recv[...].reshape(half, LANES).T
    second_nav = y_nav_recv[...].reshape(half, LANES).T
    nav = jnp.concatenate([first_nav[:8], second_nav[:8]], axis=1)
    inl_ids, xl_ids, cls_ids, live = nav[0:1], nav[1:2], nav[2:3], nav[3:4]

    seen = jnp.max(first_nav[5:6], axis=1, keepdims=True)
    flag_send[...] = jnp.broadcast_to(seen, (BLOCK_TR, LANES))
    flag_recv[0] = flag_send[...]
    for step in range(1, n_xl):
        other = lax.rem(band + step, n_xl)
        push(flag_send, flag_recv.at[step], (flag_sems.at[0, step], flag_sems.at[1, step]), {"xl": other})

    weights = jnp.zeros((TAPS, depth), jnp.float32)
    for phase in range(PHASES):
        weights = jnp.where(cls_ids == float(phase), taps_ref[:, phase : phase + 1], weights)
    weights = weights * live
    tap_of = lax.broadcasted_iota(jnp.int32, (padded, depth), 0).astype(jnp.float32) - (xl_ids + 5.0)
    spread = jnp.zeros((padded, depth), jnp.float32)
    for tap in range(TAPS):
        spread = jnp.where(tap_of == float(tap), weights[tap : tap + 1], spread)

    def line(i, carry):
        rows = jnp.where(inl_ids == i.astype(jnp.float32), spread, 0.0)
        sums = jnp.broadcast_to(jnp.sum(rows, axis=1, keepdims=True), (padded, LANES))
        base = pl.multiple_of(i * width, width)
        inner[pl.ds(base, width), :] = rows[TAPS : TAPS + width].astype(jnp.bfloat16)
        fold_in[pl.ds(base, width), :] = sums[TAPS : TAPS + width]
        edge = pl.multiple_of(i * TAPS, TAPS)
        outer_f32[0, pl.ds(edge, TAPS), :] = rows[:TAPS]
        outer_f32[1, pl.ds(edge, TAPS), :] = rows[TAPS + width :]
        fold_send[0, pl.ds(edge, TAPS), :] = sums[:TAPS]
        fold_send[1, pl.ds(edge, TAPS), :] = sums[TAPS + width :]
        return carry

    lax.fori_loop(0, IL_DEV, line, 0)
    outer[...] = outer_f32[...].astype(jnp.bfloat16).reshape(2 * side, depth)

    for way, neighbour in ((0, left), (1, right)):
        push(
            fold_send.at[way],
            fold_recv.at[way],
            (fold_sems.at[0, way], fold_sems.at[1, way]),
            {"xl": neighbour},
        )

    from_right = jnp.where(band < n_xl - 1, 1.0, 0.0)
    from_left = jnp.where(band > 0, 1.0, 0.0)

    spread_second(2)
    push_first(3)

    for way in range(2):
        wait_for(fold_recv.at[way], fold_sems.at[1, way])

    def join(i, carry):
        edge = pl.multiple_of(i * TAPS, TAPS)
        first = pl.multiple_of(i * width, TAPS)
        last = pl.multiple_of(i * width + width - TAPS, TAPS)
        fold_in[pl.ds(last, TAPS), :] += fold_recv[0, pl.ds(edge, TAPS), :] * from_right
        fold_in[pl.ds(first, TAPS), :] += fold_recv[1, pl.ds(edge, TAPS), :] * from_left
        return carry

    lax.fori_loop(0, IL_DEV, join, 0)
    fold_in[...] = 1.0 / jnp.maximum(fold_in[...], 0.25)

    for step in range(1, n_xl):
        wait_for(flag_recv.at[step], flag_sems.at[1, step])
    flag_ref[...] = jnp.max(flag_recv[...], axis=0)

    def stage(c):
        lo, hi = span_of(c, length)
        size = hi - lo
        wait_for(y_recv.at[pl.ds(0, plane - 1), :, span(c)], y_sems.at[1, c])
        samples_in[half:, :size] = y_recv[:, :, lo:hi].reshape(half, size).astype(jnp.bfloat16)
        wait_for(p_recv.at[pl.ds(0, n_inl - 1), :, span(c)], p_sems.at[1, c])
        samples_in[:half, :size] = p_recv[:, :, lo:hi].reshape(half, size).astype(jnp.bfloat16)
        halo_send[:, :, lo:hi] = jnp.dot(
            outer[...], samples_in[:, :size], preferred_element_type=jnp.float32
        ).reshape(2, side, size)
        for way, neighbour in ((0, left), (1, right)):
            push(
                halo_send.at[way, :, span(c)],
                halo_recv.at[way, :, span(c)],
                (halo_sems.at[0, c, way], halo_sems.at[1, c, way]),
                {"xl": neighbour},
            )
        stack[:, lo:hi] = jnp.dot(
            inner[...], samples_in[:, :size], preferred_element_type=jnp.float32
        )

    def finish(c):
        lo, hi = span_of(c, length)
        for way in range(2):
            wait_for(halo_recv.at[way, :, span(c)], halo_sems.at[1, c, way])
        tile = 2 * width

        def body(m, carry):
            base = pl.multiple_of(m * tile, tile)
            for i in range(2):
                edge = pl.multiple_of(m * 2 * TAPS + i * TAPS, TAPS)
                first = pl.multiple_of(base + i * width, TAPS)
                last = pl.multiple_of(base + i * width + width - TAPS, TAPS)
                stack[pl.ds(last, TAPS), lo:hi] += halo_recv[0, pl.ds(edge, TAPS), lo:hi] * from_right
                stack[pl.ds(first, TAPS), lo:hi] += halo_recv[1, pl.ds(edge, TAPS), lo:hi] * from_left
            scale = fold_in[pl.ds(base, tile), 0:1]
            binned = (stack[pl.ds(base, tile), lo:hi] * scale).astype(jnp.bfloat16)
            if c == PARTS - 1:
                binned_ref[pl.ds(base, tile), :] = binned
                return carry
            part = jnp.dot(binned, resample[lo:hi, :], preferred_element_type=jnp.float32)
            if c > 0:
                part = part + total[pl.ds(base, tile), :]
            total[pl.ds(base, tile), :] = part
            return carry

        lax.fori_loop(0, IL_DEV // 2, body, 0)

    stage(0)
    finish(0)
    stage(1)
    spread_second(3)
    finish(1)
    stage(2)
    stage(3)
    finish(2)
    finish(3)

    wait_for(p_nav_send.at[pl.ds(0, n_inl - 1)], nav_sems.at[0, 0])
    wait_for(z_nav_send.at[pl.ds(0, layers - 1)], nav_sems.at[0, 1])
    wait_for(y_nav_send.at[pl.ds(0, plane - 1)], nav_sems.at[0, 2])
    for c in range(PARTS):
        wait_for(p_send.at[pl.ds(0, n_inl - 1), :, span(c)], p_sems.at[0, c])
        wait_for(z_send.at[pl.ds(0, layers - 1), :, span(c)], z_sems.at[0, c])
        wait_for(y_send.at[pl.ds(0, plane - 1), :, span(c)], y_sems.at[0, c])
        for way in range(2):
            wait_for(halo_send.at[way, :, span(c)], halo_sems.at[0, c, way])
    for way in range(2):
        wait_for(fold_send.at[way], fold_sems.at[0, way])
    for step in range(1, n_xl):
        wait_for(flag_send, flag_sems.at[0, step])


def finish_kernel(total_ref, binned_ref, tail_ref, out_hbm, rows, sem):
    tile = rows.shape[0] // 8

    def body(m, carry):
        base = pl.multiple_of(m * tile, tile)
        part = jnp.dot(
            binned_ref[pl.ds(base, tile), :], tail_ref[...], preferred_element_type=jnp.float32
        )
        rows[pl.ds(base, tile), :] = (total_ref[pl.ds(base, tile), :] + part).astype(jnp.bfloat16)
        pltpu.make_async_copy(
            rows.at[pl.ds(base, tile)], out_hbm.at[pl.ds(base, tile)], sem
        ).start()
        return carry

    lax.fori_loop(0, 8, body, 0)
    wait_for(rows, sem)


def pass_kernel(in_ref, out_ref):
    out_ref[...] = in_ref[...]


def per_device(traces, owner, counts, inline_off, xline_off, phase_cls):
    n_inl, n_xl = lax.axis_size("inl"), lax.axis_size("xl")
    plane = plane_of(n_inl)
    layers = n_inl // plane
    local_blocks, _, samples = traces.shape
    width = XLINES // n_xl
    large = widest(samples)
    last = span_of(PARTS - 1, samples)[1] - span_of(PARTS - 1, samples)[0]
    half = n_inl * BLOCK_TR
    side = IL_DEV * TAPS
    rows = IL_DEV * width
    in_vmem = pl.BlockSpec(memory_space=pltpu.VMEM)
    in_smem = pl.BlockSpec(memory_space=pltpu.SMEM)
    anywhere = pl.BlockSpec(memory_space=pl.ANY)
    table, nav, taps = pl.pallas_call(
        functools.partial(plan_kernel, n_inl),
        out_shape=(
            jax.ShapeDtypeStruct((n_inl + 8, LANES), jnp.int32),
            jax.ShapeDtypeStruct((local_blocks + 1, BLOCK_TR, LANES), jnp.float32),
            jax.ShapeDtypeStruct((TAPS, LANES), jnp.float32),
        ),
        in_specs=[in_vmem] * 5,
        out_specs=(in_vmem, in_vmem, in_vmem),
        compiler_params=pltpu.CompilerParams(vmem_limit_bytes=8 << 20),
    )(
        owner.reshape(1, local_blocks),
        counts.reshape(1, local_blocks),
        inline_off.T,
        xline_off.T,
        phase_cls.T,
    )
    f32, bf16 = jnp.float32, jnp.bfloat16
    scratch = [
        pltpu.VMEM((local_blocks, BLOCK_TR, samples), f32),
        pltpu.VMEM((n_inl, BLOCK_TR, samples), f32),
        pltpu.VMEM((n_inl, BLOCK_TR, samples), f32),
        pltpu.VMEM((layers, CAP * BLOCK_TR, samples), f32),
        pltpu.VMEM((layers, CAP * BLOCK_TR, samples), f32),
        pltpu.VMEM((plane, layers * BLOCK_TR, samples), f32),
        pltpu.VMEM((plane, layers * BLOCK_TR, samples), f32),
        pltpu.VMEM((n_inl, BLOCK_TR, LANES), f32),
        pltpu.VMEM((n_inl, BLOCK_TR, LANES), f32),
        pltpu.VMEM((layers, CAP, BLOCK_TR, LANES), f32),
        pltpu.VMEM((layers, CAP, BLOCK_TR, LANES), f32),
        pltpu.VMEM((plane, layers, BLOCK_TR, LANES), f32),
        pltpu.VMEM((plane, layers, BLOCK_TR, LANES), f32),
        pltpu.VMEM((2 * half, large), bf16),
        pltpu.VMEM((rows, 2 * half), bf16),
        pltpu.VMEM((2, side, 2 * half), f32),
        pltpu.VMEM((2 * side, 2 * half), bf16),
        pltpu.VMEM((samples, 2 * samples), bf16),
        pltpu.VMEM((rows, samples), f32),
        pltpu.VMEM((2, side, samples), f32),
        pltpu.VMEM((2, side, samples), f32),
        pltpu.VMEM((rows, LANES), f32),
        pltpu.VMEM((2, side, LANES), f32),
        pltpu.VMEM((2, side, LANES), f32),
        pltpu.VMEM((BLOCK_TR, LANES), f32),
        pltpu.VMEM((n_xl, BLOCK_TR, LANES), f32),
        pltpu.SemaphoreType.DMA,
        pltpu.SemaphoreType.DMA((2, PARTS)),
        pltpu.SemaphoreType.DMA((2, PARTS)),
        pltpu.SemaphoreType.DMA((2, PARTS)),
        pltpu.SemaphoreType.DMA((2, 3)),
        pltpu.SemaphoreType.DMA((2, PARTS, 2)),
        pltpu.SemaphoreType.DMA((2, 2)),
        pltpu.SemaphoreType.DMA((2, n_xl)),
    ]
    total, tail, binned, flag = pl.pallas_call(
        functools.partial(fast_kernel, n_inl, n_xl),
        out_shape=(
            jax.ShapeDtypeStruct((rows, 2 * samples), f32),
            jax.ShapeDtypeStruct((last, 2 * samples), bf16),
            jax.ShapeDtypeStruct((rows, last), bf16),
            jax.ShapeDtypeStruct((BLOCK_TR, LANES), f32),
        ),
        in_specs=[in_smem, anywhere, in_vmem, in_vmem],
        out_specs=(in_vmem, in_vmem, in_vmem, in_vmem),
        scratch_shapes=scratch,
        compiler_params=pltpu.CompilerParams(
            collective_id=0, has_side_effects=True, vmem_limit_bytes=36 << 20
        ),
    )(table, traces, nav, taps)

    def finish_fast():
        out = pl.pallas_call(
            finish_kernel,
            out_shape=jax.ShapeDtypeStruct((rows, 2 * samples), bf16),
            in_specs=[in_vmem] * 3,
            out_specs=pl.BlockSpec(memory_space=pltpu.HBM),
            scratch_shapes=[pltpu.VMEM((rows, 2 * samples), bf16), pltpu.SemaphoreType.DMA],
            compiler_params=pltpu.CompilerParams(vmem_limit_bytes=53 << 20),
        )(total, binned, tail)
        return out.reshape(IL_DEV, width, 2 * samples)

    def run_padded():
        out = padded_plan(traces, owner, counts, inline_off, xline_off, phase_cls)
        spec = pl.BlockSpec((2, width, 2 * samples), lambda m: (m, 0, 0))
        return pl.pallas_call(
            pass_kernel,
            grid=(IL_DEV // 2,),
            out_shape=jax.ShapeDtypeStruct(out.shape, out.dtype),
            in_specs=[spec],
            out_specs=spec,
            compiler_params=pltpu.CompilerParams(vmem_limit_bytes=12 << 20),
        )(out)

    return lax.cond(flag[0, 0] > 0.5, run_padded, finish_fast)


def solution(mesh):
    return jax.shard_map(
        per_device,
        mesh=mesh,
        in_specs=(
            P(("inl", "xl"), None, None),
            P(("inl", "xl"), None),
            P(("inl", "xl")),
            P(("inl", "xl"), None),
            P(("inl", "xl"), None),
            P(("inl", "xl"), None),
        ),
        out_specs=P("inl", "xl", None),
        check_vma=False,
    )
```

```python
import functools
import math

import jax
import jax.numpy as jnp
from jax import lax
from jax.experimental import pallas as pl
from jax.experimental.pallas import tpu as pltpu
from jax.sharding import PartitionSpec as P

XLINES = 256
TAPS = 8
PHASES = 16
BLOCK_TR = 8
SLOTS = 2
IL_DEV = 16
CHUNKS = 4
CAP = 3
LANES = 128
ROWS = SLOTS * BLOCK_TR
MESH = pl.DeviceIdType.MESH


def sinc_table():
    phase_idx = jnp.arange(PHASES, dtype=jnp.int32).astype(jnp.float32)[:, None]
    tap_idx = jnp.arange(TAPS, dtype=jnp.int32).astype(jnp.float32)[None, :]
    offset = tap_idx - 3.0 - phase_idx / PHASES
    return jnp.sinc(offset) * (0.5 + 0.5 * jnp.cos(math.pi * offset / 4.0))


def wait_for(ref, sem):
    pltpu.make_async_copy(ref, ref, sem).wait()


def build_resample(table_ref):
    length, width = table_ref.shape
    step = 16

    def body(part, carry):
        base = pl.multiple_of(part * step, step)
        rows_idx = lax.broadcasted_iota(jnp.int32, (step, width), 0) + base
        cols_idx = lax.broadcasted_iota(jnp.int32, (step, width), 1)
        lagged = (cols_idx >> 1) - rows_idx
        sign_val = (1 - 2 * (lagged & 1)).astype(jnp.float32)
        odd_val = sign_val / (math.pi * (lagged.astype(jnp.float32) + 0.5))
        even_val = (lagged == 0).astype(jnp.float32)
        table_ref[pl.ds(base, step), :] = jnp.where((cols_idx & 1) == 1, odd_val, even_val).astype(
            jnp.bfloat16
        )
        return carry

    lax.fori_loop(0, length // step, body, 0)


def padded_kernel(
    n_inl,
    n_xl,
    index_ref,
    traces_hbm,
    nav_ref,
    taps_ref,
    out_hbm,
    traces,
    send,
    recv,
    nav_send,
    nav_recv,
    inner,
    outer_f32,
    outer,
    resample,
    total,
    stack,
    out_rows,
    halo_send,
    halo_recv,
    fold_in,
    fold_send,
    fold_recv,
    load_sem,
    send_sems,
    recv_sems,
    nav_send_sem,
    nav_recv_sem,
    halo_send_sems,
    halo_recv_sems,
    fold_send_sems,
    fold_recv_sems,
    out_sem,
):
    me = lax.axis_index("inl")
    band = lax.axis_index("xl")
    right, left = lax.rem(band + 1, n_xl), lax.rem(band + n_xl - 1, n_xl)
    chunk = traces.shape[2] // CHUNKS
    depth = n_inl * ROWS
    width = inner.shape[0] // IL_DEV
    padded = width + 2 * TAPS
    side = IL_DEV * TAPS

    load = pltpu.make_async_copy(traces_hbm, traces, load_sem)
    load.start()

    barrier = pltpu.get_barrier_semaphore()

    def greet(off, carry):
        dest = lax.rem(me + off, n_inl)
        pl.semaphore_signal(barrier, inc=1, device_id={"inl": dest}, device_id_type=MESH)
        return carry

    lax.fori_loop(1, n_inl, greet, 0)
    for neighbour in (left, right):
        pl.semaphore_signal(barrier, inc=1, device_id={"xl": neighbour}, device_id_type=MESH)

    def gather_nav(off, carry):
        dest = lax.rem(me + off, n_inl)
        for slot in range(SLOTS):
            block = index_ref[dest, slot]
            nav_send[dest, slot * BLOCK_TR : (slot + 1) * BLOCK_TR, :] = nav_ref[block]
        return carry

    lax.fori_loop(0, n_inl, gather_nav, 0)
    nav_recv[me] = nav_send[me]
    load.wait()

    def gather(c):
        def body(off, carry):
            dest = lax.rem(me + off, n_inl)
            for slot in range(SLOTS):
                block = index_ref[dest, SLOTS + slot]
                send[c, dest, slot * BLOCK_TR : (slot + 1) * BLOCK_TR, :] = traces[
                    block, :, c * chunk : (c + 1) * chunk
                ]
            return carry

        lax.fori_loop(0, n_inl, body, 0)
        recv[c, me] = send[c, me]

    gather(0)
    pl.semaphore_wait(barrier, n_inl - 1 + 2)

    def push_nav(off, carry):
        dest = lax.rem(me + off, n_inl)
        pltpu.make_async_remote_copy(
            src_ref=nav_send.at[dest],
            dst_ref=nav_recv.at[me],
            send_sem=nav_send_sem,
            recv_sem=nav_recv_sem,
            device_id={"inl": dest},
            device_id_type=MESH,
        ).start()
        return carry

    lax.fori_loop(1, n_inl, push_nav, 0)

    def push(c):
        def body(off, carry):
            dest = lax.rem(me + off, n_inl)
            pltpu.make_async_remote_copy(
                src_ref=send.at[c, dest],
                dst_ref=recv.at[c, me],
                send_sem=send_sems.at[c],
                recv_sem=recv_sems.at[c],
                device_id={"inl": dest},
                device_id_type=MESH,
            ).start()
            return carry

        lax.fori_loop(1, n_inl, body, 0)

    for c in range(CHUNKS):
        if c + 1 < CHUNKS:
            gather(c + 1)
        push(c)

    build_resample(resample)

    wait_for(nav_recv.at[pl.ds(0, n_inl - 1)], nav_recv_sem)
    nav = nav_recv[...].reshape(depth, LANES).T
    inl_ids, xl_ids, cls_ids, live = nav[0:1], nav[1:2], nav[2:3], nav[3:4]
    weights = jnp.zeros((TAPS, depth), jnp.float32)
    for phase in range(PHASES):
        weights = jnp.where(cls_ids == float(phase), taps_ref[:, phase : phase + 1], weights)
    weights = weights * live
    tap_of = lax.broadcasted_iota(jnp.int32, (padded, depth), 0).astype(jnp.float32) - (xl_ids + 5.0)
    spread = jnp.zeros((padded, depth), jnp.float32)
    for tap in range(TAPS):
        spread = jnp.where(tap_of == float(tap), weights[tap : tap + 1], spread)

    def line(i, carry):
        rows = jnp.where(inl_ids == i.astype(jnp.float32), spread, 0.0)
        sums = jnp.broadcast_to(jnp.sum(rows, axis=1, keepdims=True), (padded, LANES))
        base = pl.multiple_of(i * width, width)
        inner[pl.ds(base, width), :] = rows[TAPS : TAPS + width].astype(jnp.bfloat16)
        fold_in[pl.ds(base, width), :] = sums[TAPS : TAPS + width]
        edge = pl.multiple_of(i * TAPS, TAPS)
        outer_f32[0, pl.ds(edge, TAPS), :] = rows[:TAPS]
        outer_f32[1, pl.ds(edge, TAPS), :] = rows[TAPS + width :]
        fold_send[0, pl.ds(edge, TAPS), :] = sums[:TAPS]
        fold_send[1, pl.ds(edge, TAPS), :] = sums[TAPS + width :]
        return carry

    lax.fori_loop(0, IL_DEV, line, 0)
    outer[...] = outer_f32[...].astype(jnp.bfloat16).reshape(2 * side, depth)

    folds = []
    for way, neighbour in ((0, left), (1, right)):
        copy = pltpu.make_async_remote_copy(
            src_ref=fold_send.at[way],
            dst_ref=fold_recv.at[way],
            send_sem=fold_send_sems.at[way],
            recv_sem=fold_recv_sems.at[way],
            device_id={"xl": neighbour},
            device_id_type=MESH,
        )
        copy.start()
        folds.append(copy)

    from_right = jnp.where(band < n_xl - 1, 1.0, 0.0)
    from_left = jnp.where(band > 0, 1.0, 0.0)

    for copy in folds:
        copy.wait()

    def join(i, carry):
        edge = pl.multiple_of(i * TAPS, TAPS)
        first = pl.multiple_of(i * width, TAPS)
        last = pl.multiple_of(i * width + width - TAPS, TAPS)
        fold_in[pl.ds(last, TAPS), :] += fold_recv[0, pl.ds(edge, TAPS), :] * from_right
        fold_in[pl.ds(first, TAPS), :] += fold_recv[1, pl.ds(edge, TAPS), :] * from_left
        return carry

    lax.fori_loop(0, IL_DEV, join, 0)
    fold_in[...] = 1.0 / jnp.maximum(fold_in[...], 0.25)

    halos = []
    for c in range(CHUNKS):
        wait_for(recv.at[c, pl.ds(0, n_inl - 1)], recv_sems.at[c])
        block = recv[c].reshape(depth, chunk).astype(jnp.bfloat16)
        halo_send[c] = jnp.dot(outer[...], block, preferred_element_type=jnp.float32).reshape(
            2, side, chunk
        )
        stack[...] = jnp.dot(inner[...], block, preferred_element_type=jnp.float32)
        sent = []
        for way, neighbour in ((0, left), (1, right)):
            copy = pltpu.make_async_remote_copy(
                src_ref=halo_send.at[c, way],
                dst_ref=halo_recv.at[c, way],
                send_sem=halo_send_sems.at[c, way],
                recv_sem=halo_recv_sems.at[c, way],
                device_id={"xl": neighbour},
                device_id_type=MESH,
            )
            copy.start()
            sent.append(copy)
        for copy in sent:
            copy.wait()

        def add_halo(i, carry, c=c):
            edge = pl.multiple_of(i * TAPS, TAPS)
            first = pl.multiple_of(i * width, TAPS)
            last = pl.multiple_of(i * width + width - TAPS, TAPS)
            stack[pl.ds(last, TAPS), :] += halo_recv[c, 0, pl.ds(edge, TAPS), :] * from_right
            stack[pl.ds(first, TAPS), :] += halo_recv[c, 1, pl.ds(edge, TAPS), :] * from_left
            return carry

        lax.fori_loop(0, IL_DEV, add_halo, 0)

        tile = out_rows.shape[0] // TAPS

        def finish(m, carry, c=c):
            base = pl.multiple_of(m * tile, tile)
            scale = fold_in[pl.ds(base, tile), 0:1]
            binned = (stack[pl.ds(base, tile), :] * scale).astype(jnp.bfloat16)
            part = jnp.dot(
                binned, resample[c * chunk : (c + 1) * chunk, :], preferred_element_type=jnp.float32
            )
            if c > 0:
                part = part + total[pl.ds(base, tile), :]
            if c < CHUNKS - 1:
                total[pl.ds(base, tile), :] = part
            else:
                out_rows[pl.ds(base, tile), :] = part.astype(jnp.bfloat16)
                pltpu.make_async_copy(
                    out_rows.at[pl.ds(base, tile)], out_hbm.at[pl.ds(base, tile)], out_sem
                ).start()
            return carry

        lax.fori_loop(0, TAPS, finish, 0)

    wait_for(nav_send.at[pl.ds(0, n_inl - 1)], nav_send_sem)
    for c in range(CHUNKS):
        wait_for(send.at[c, pl.ds(0, n_inl - 1)], send_sems.at[c])
    wait_for(out_rows, out_sem)


def padded_plan(traces, owner, counts, inline_off, xline_off, phase_cls):
    n_inl, n_xl = lax.axis_size("inl"), lax.axis_size("xl")
    local_blocks, _, samples = traces.shape
    width = XLINES // n_xl
    chunk = samples // CHUNKS
    depth = n_inl * ROWS
    side = IL_DEV * TAPS
    block_idx = jnp.arange(local_blocks, dtype=jnp.int32)
    named = owner[:, 0][None, :] == jnp.arange(n_inl, dtype=jnp.int32)[:, None]
    low = jnp.min(jnp.where(named, block_idx[None, :], local_blocks), axis=1)
    high = jnp.max(jnp.where(named, block_idx[None, :], -1), axis=1)
    high = jnp.where(high > low, high, local_blocks)
    nav_index = jnp.stack([low, high], axis=1)
    index = jnp.concatenate([nav_index, jnp.minimum(nav_index, local_blocks - 1)], axis=1)
    live = (jnp.arange(BLOCK_TR, dtype=jnp.int32)[None, :] < counts[:, None]).astype(jnp.float32)
    parts = [inline_off.astype(jnp.float32), xline_off.astype(jnp.float32)]
    parts = parts + [phase_cls.astype(jnp.float32), live]
    nav = jnp.stack(parts, axis=2)
    nav = jnp.pad(nav, ((0, 1), (0, 0), (0, LANES - len(parts))))
    taps = sinc_table().T
    scratch = [
        pltpu.VMEM((local_blocks, BLOCK_TR, samples), jnp.float32),
        pltpu.VMEM((CHUNKS, n_inl, ROWS, chunk), jnp.float32),
        pltpu.VMEM((CHUNKS, n_inl, ROWS, chunk), jnp.float32),
        pltpu.VMEM((n_inl, ROWS, LANES), jnp.float32),
        pltpu.VMEM((n_inl, ROWS, LANES), jnp.float32),
        pltpu.VMEM((IL_DEV * width, depth), jnp.bfloat16),
        pltpu.VMEM((2, side, depth), jnp.float32),
        pltpu.VMEM((2 * side, depth), jnp.bfloat16),
        pltpu.VMEM((samples, 2 * samples), jnp.bfloat16),
        pltpu.VMEM((IL_DEV * width, 2 * samples), jnp.float32),
        pltpu.VMEM((IL_DEV * width, chunk), jnp.float32),
        pltpu.VMEM((IL_DEV * width, 2 * samples), jnp.bfloat16),
        pltpu.VMEM((CHUNKS, 2, side, chunk), jnp.float32),
        pltpu.VMEM((CHUNKS, 2, side, chunk), jnp.float32),
        pltpu.VMEM((IL_DEV * width, LANES), jnp.float32),
        pltpu.VMEM((2, side, LANES), jnp.float32),
        pltpu.VMEM((2, side, LANES), jnp.float32),
        pltpu.SemaphoreType.DMA,
        pltpu.SemaphoreType.DMA((CHUNKS,)),
        pltpu.SemaphoreType.DMA((CHUNKS,)),
        pltpu.SemaphoreType.DMA,
        pltpu.SemaphoreType.DMA,
        pltpu.SemaphoreType.DMA((CHUNKS, 2)),
        pltpu.SemaphoreType.DMA((CHUNKS, 2)),
        pltpu.SemaphoreType.DMA((2,)),
        pltpu.SemaphoreType.DMA((2,)),
        pltpu.SemaphoreType.DMA,
    ]
    out = pl.pallas_call(
        functools.partial(padded_kernel, n_inl, n_xl),
        out_shape=jax.ShapeDtypeStruct((IL_DEV * width, 2 * samples), jnp.bfloat16),
        in_specs=[
            pl.BlockSpec(memory_space=pltpu.SMEM),
            pl.BlockSpec(memory_space=pl.ANY),
            pl.BlockSpec(memory_space=pltpu.VMEM),
            pl.BlockSpec(memory_space=pltpu.VMEM),
        ],
        out_specs=pl.BlockSpec(memory_space=pl.ANY),
        scratch_shapes=scratch,
        compiler_params=pltpu.CompilerParams(
            collective_id=1, has_side_effects=True, vmem_limit_bytes=44 << 20
        ),
    )(index, traces, nav, taps)
    return out.reshape(IL_DEV, width, 2 * samples)


OWN_LANE = 4 * BLOCK_TR
OVER_LANE = OWN_LANE + 1
EDGES = (0, 3, 5, 7, 8)
PARTS = len(EDGES) - 1


def span_of(c, length):
    return EDGES[c] * length // EDGES[-1], EDGES[c + 1] * length // EDGES[-1]


def widest(length):
    return max(hi - lo for lo, hi in [span_of(c, length) for c in range(PARTS)])


def plane_of(n_inl):
    return 8 if n_inl % 8 == 0 and n_inl > 8 else 2


def plan_kernel(n_inl, owner_ref, counts_ref, inl_ref, xl_ref, cls_ref, table_ref, nav_ref, taps_ref):
    blocks = owner_ref.shape[1]
    plane = plane_of(n_inl)
    named = owner_ref[...] == lax.broadcasted_iota(jnp.int32, (n_inl, blocks), 0)
    block_idx = lax.broadcasted_iota(jnp.int32, (n_inl, blocks), 1).astype(jnp.float32)
    low = jnp.min(jnp.where(named, block_idx, float(blocks)), axis=1, keepdims=True)
    high = jnp.max(jnp.where(named, block_idx, -1.0), axis=1, keepdims=True)
    two = jnp.broadcast_to(jnp.where(high > low, 1.0, 0.0), (n_inl, LANES))
    row_id = lax.broadcasted_iota(jnp.int32, (n_inl, n_inl), 0)
    col_id = lax.broadcasted_iota(jnp.int32, (n_inl, n_inl), 1)
    ahead = jnp.where((col_id < row_id) & (col_id // plane == row_id // plane), 1.0, 0.0)
    rank = jnp.dot(ahead, two, preferred_element_type=jnp.float32)
    own = lax.broadcasted_iota(jnp.int32, (n_inl, LANES), 0)
    lane = lax.broadcasted_iota(jnp.int32, (n_inl, LANES), 1)
    slot = (own // plane * CAP).astype(jnp.float32) + rank
    chosen = (two > 0.5) & (rank < CAP - 0.5) & (slot == lane.astype(jnp.float32))
    taken = jnp.sum(jnp.where(chosen, 1.0, 0.0), axis=0, keepdims=True)
    second = jnp.sum(jnp.where(chosen, high, 0.0), axis=0, keepdims=True)
    second = jnp.where(taken > 0.5, second, float(blocks))
    target = jnp.where(chosen, (own % plane + 1).astype(jnp.float32), 0.0)
    target = jnp.sum(target, axis=0, keepdims=True)
    over = jnp.where((two > 0.5) & (rank > CAP - 0.5), 1.0, 0.0)
    over = jnp.max(over, axis=0, keepdims=True)
    table_ref[:n_inl, :] = jnp.broadcast_to(low, (n_inl, LANES)).astype(jnp.int32)
    table_ref[n_inl : n_inl + 1, :] = second.astype(jnp.int32)
    table_ref[n_inl + 1 : n_inl + 2, :] = target.astype(jnp.int32)
    table_ref[n_inl + 2 : n_inl + 3, :] = over.astype(jnp.int32)
    table_ref[n_inl + 3 :, :] = jnp.zeros((5, LANES), jnp.int32)
    tap = lax.broadcasted_iota(jnp.int32, (TAPS, LANES), 0).astype(jnp.float32)
    offset = tap - 3.0 - lax.broadcasted_iota(jnp.int32, (TAPS, LANES), 1).astype(jnp.float32) / PHASES
    at_zero = offset == 0.0
    angle = math.pi * jnp.where(at_zero, 1.0, offset)
    sinc = jnp.where(at_zero, 1.0, jnp.sin(angle) / angle)
    taps_ref[...] = sinc * (0.5 + 0.5 * jnp.cos(math.pi * offset / 4.0))
    trace_idx = lax.broadcasted_iota(jnp.int32, (BLOCK_TR, blocks), 0)
    fields = [inl_ref[...], xl_ref[...], cls_ref[...], (trace_idx < counts_ref[...]).astype(jnp.int32)]
    fields = [field.astype(jnp.float32) for field in fields]
    unused = jnp.zeros((LANES - len(fields) * BLOCK_TR, blocks), jnp.float32)
    columns = jnp.concatenate(fields + [unused], axis=0)
    same_row = lax.broadcasted_iota(jnp.int32, (blocks, blocks), 0)
    same_col = lax.broadcasted_iota(jnp.int32, (blocks, blocks), 1)
    flat = lax.dot_general(
        jnp.where(same_row == same_col, 1.0, 0.0),
        columns,
        (((1,), (1,)), ((), ())),
        preferred_element_type=jnp.float32,
    )
    for block in range(blocks):
        nav_ref[block] = flat[block : block + 1]
    nav_ref[blocks] = jnp.zeros((1, LANES), jnp.float32)


def fast_kernel(
    n_inl,
    n_xl,
    table_ref,
    traces_hbm,
    nav_ref,
    taps_ref,
    total,
    tail_ref,
    binned_ref,
    flag_ref,
    traces,
    p_send,
    p_recv,
    z_send,
    z_recv,
    y_send,
    y_recv,
    p_nav_send,
    p_nav_recv,
    z_nav_send,
    z_nav_recv,
    y_nav_send,
    y_nav_recv,
    z_own,
    nav_rows,
    samples_in,
    inner,
    outer_f32,
    outer,
    resample,
    stack,
    halo_send,
    halo_recv,
    fold_in,
    fold_send,
    fold_recv,
    flag_send,
    flag_recv,
    load_sem,
    p_sems,
    z_sems,
    y_sems,
    nav_sems,
    halo_sems,
    fold_sems,
    flag_sems,
):
    me = lax.axis_index("inl")
    band = lax.axis_index("xl")
    plane = plane_of(n_inl)
    layers = n_inl // plane
    layer, place = me // plane, lax.rem(me, plane)
    right, left = lax.rem(band + 1, n_xl), lax.rem(band + n_xl - 1, n_xl)
    length = traces.shape[2]
    blocks = traces.shape[0]
    half = n_inl * BLOCK_TR
    depth = 2 * half
    width = inner.shape[0] // IL_DEV
    padded = width + 2 * TAPS
    side = IL_DEV * TAPS

    load = pltpu.make_async_copy(traces_hbm, traces, load_sem)
    load.start()

    barrier = pltpu.get_barrier_semaphore()

    def greet(off, carry):
        dest = lax.rem(me + 1 + lax.rem(off + n_inl * 7 // 16, n_inl - 1), n_inl)
        pl.semaphore_signal(barrier, inc=1, device_id={"inl": dest}, device_id_type=MESH)
        return carry

    lax.fori_loop(0, n_inl - 1, greet, 0)
    for step in range(1, n_xl):
        other = lax.rem(band + step, n_xl)
        pl.semaphore_signal(barrier, inc=1, device_id={"xl": other}, device_id_type=MESH)

    field_id = lax.broadcasted_iota(jnp.int32, (1, LANES), 1)
    over = table_ref[n_inl + 2, 0].astype(jnp.float32)
    load.wait()

    def gather_second(layer_to, carry):
        for r in range(CAP):
            spot = layer_to * CAP + r
            block = table_ref[n_inl, spot]
            target = table_ref[n_inl + 1, spot].astype(jnp.float32)
            z_nav_send[layer_to, r] = jnp.where(field_id == OWN_LANE, target, nav_ref[block])
            z_send[layer_to, r * BLOCK_TR : (r + 1) * BLOCK_TR, :] = traces[
                jnp.minimum(block, blocks - 1)
            ]
        return carry

    lax.fori_loop(0, layers, gather_second, 0)

    def gather_first(off, carry):
        dest = lax.rem(me + off, n_inl)
        block = table_ref[dest, 0]
        p_nav_send[dest] = jnp.where(field_id == OVER_LANE, over, nav_ref[block])
        p_send[dest] = traces[jnp.minimum(block, blocks - 1)]
        return carry

    lax.fori_loop(0, n_inl, gather_first, 0)
    p_nav_recv[me] = p_nav_send[me]
    p_recv[me] = p_send[me]
    z_nav_recv[layer] = z_nav_send[layer]
    z_recv[layer] = z_send[layer]

    pl.semaphore_wait(barrier, n_inl - 1 + n_xl - 1)

    def span(c):
        lo, hi = span_of(c, length)
        return pl.ds(lo, hi - lo)

    def away(off):
        reach = (off + 1) // 2
        return lax.rem(layer + jnp.where(lax.rem(off, 2) == 1, reach, layers - reach), layers)

    def partner(off):
        return away(lax.rem(off, layers)) * plane + lax.rem(place + off // layers, plane)

    def push(source, target, sems, to):
        pltpu.make_async_remote_copy(
            src_ref=source,
            dst_ref=target,
            send_sem=sems[0],
            recv_sem=sems[1],
            device_id=to,
            device_id_type=MESH,
        ).start()

    def push_first(c):
        def body(off, carry):
            dest = partner(off)
            push(
                p_send.at[dest, :, span(c)],
                p_recv.at[me, :, span(c)],
                (p_sems.at[0, c], p_sems.at[1, c]),
                {"inl": dest},
            )
            return carry

        lax.fori_loop(1, n_inl, body, 0)

    def push_second(c):
        def body(off, carry):
            to = away(off)
            push(
                z_send.at[to, :, span(c)],
                z_recv.at[layer, :, span(c)],
                (z_sems.at[0, c], z_sems.at[1, c]),
                {"inl": to * plane + place},
            )
            return carry

        lax.fori_loop(1, layers, body, 0)

    def spread_second(c):
        lo, hi = span_of(c, length)
        wait_for(z_recv.at[pl.ds(0, layers - 1), :, span(c)], z_sems.at[1, c])

        def body(to, carry):
            wanted = (to + 1).astype(jnp.float32)
            for origin in range(layers):
                held = jnp.zeros((BLOCK_TR, hi - lo), jnp.float32)
                for r in range(CAP):
                    named = z_own[origin, r, :, 0:1] == wanted
                    value = z_recv[origin, r * BLOCK_TR : (r + 1) * BLOCK_TR, lo:hi]
                    held = jnp.where(named, value, held)
                y_send[to, origin * BLOCK_TR : (origin + 1) * BLOCK_TR, lo:hi] = held
            return carry

        lax.fori_loop(0, plane, body, 0)
        y_recv[place, :, lo:hi] = y_send[place, :, lo:hi]

        def send(off, carry):
            to = lax.rem(place + off, plane)
            push(
                y_send.at[to, :, span(c)],
                y_recv.at[place, :, span(c)],
                (y_sems.at[0, c], y_sems.at[1, c]),
                {"inl": layer * plane + to},
            )
            return carry

        lax.fori_loop(1, plane, send, 0)

    def push_z_nav(off, carry):
        to = lax.rem(layer + off, layers)
        push(
            z_nav_send.at[to],
            z_nav_recv.at[layer],
            (nav_sems.at[0, 1], nav_sems.at[1, 1]),
            {"inl": to * plane + place},
        )
        return carry

    def push_p_nav(off, carry):
        dest = lax.rem(me + off, n_inl)
        push(
            p_nav_send.at[dest],
            p_nav_recv.at[me],
            (nav_sems.at[0, 0], nav_sems.at[1, 0]),
            {"inl": dest},
        )
        return carry

    push_second(0)
    lax.fori_loop(1, layers, push_z_nav, 0)
    push_second(1)
    push_first(0)
    lax.fori_loop(1, n_inl, push_p_nav, 0)
    push_second(2)
    push_first(1)

    wait_for(z_nav_recv.at[pl.ds(0, layers - 1)], nav_sems.at[1, 1])

    for origin in range(layers):
        for r in range(CAP):
            own = z_nav_recv[origin, r][:, OWN_LANE : OWN_LANE + 1]
            z_own[origin, r] = jnp.broadcast_to(own, (BLOCK_TR, LANES))

    def spread_nav(to, carry):
        wanted = (to + 1).astype(jnp.float32)
        for origin in range(layers):
            held = jnp.zeros((1, LANES), jnp.float32)
            for r in range(CAP):
                held = jnp.where(z_own[origin, r, 0:1, 0:1] == wanted, z_nav_recv[origin, r], held)
            y_nav_send[to, origin] = held
        return carry

    lax.fori_loop(0, plane, spread_nav, 0)
    y_nav_recv[place] = y_nav_send[place]

    def push_y_nav(off, carry):
        to = lax.rem(place + off, plane)
        push(
            y_nav_send.at[to],
            y_nav_recv.at[place],
            (nav_sems.at[0, 2], nav_sems.at[1, 2]),
            {"inl": layer * plane + to},
        )
        return carry

    lax.fori_loop(1, plane, push_y_nav, 0)
    spread_second(0)
    build_resample(resample)
    tail_ref[...] = resample[span_of(PARTS - 1, length)[0] :, :]
    spread_second(1)
    push_second(3)
    push_first(2)

    wait_for(p_nav_recv.at[pl.ds(0, n_inl - 1)], nav_sems.at[1, 0])
    wait_for(y_nav_recv.at[pl.ds(0, plane - 1)], nav_sems.at[1, 2])
    def first_row(row, carry):
        nav_rows[pl.ds(row, 1), :] = p_nav_recv[row]
        return carry

    lax.fori_loop(0, n_inl, first_row, 0)

    def second_row(origin, carry):
        for to in range(plane):
            nav_rows[pl.ds(n_inl + to * layers + origin, 1), :] = y_nav_recv[to, origin]
        return carry

    lax.fori_loop(0, layers, second_row, 0)
    column = lax.broadcasted_iota(jnp.int32, (LANES, depth), 1)
    source = lax.broadcasted_iota(jnp.int32, (LANES, depth), 0)
    owner_row = lax.broadcasted_iota(jnp.int32, (2 * n_inl, depth), 0)
    owner_col = lax.broadcasted_iota(jnp.int32, (2 * n_inl, depth), 1)
    lines = []
    for field in range(4):
        pick = jnp.where(source == field * BLOCK_TR + column % BLOCK_TR, 1.0, 0.0)
        wide = jnp.dot(nav_rows[...], pick, preferred_element_type=jnp.float32)
        mine = jnp.where(owner_row == owner_col // BLOCK_TR, wide, 0.0)
        lines.append(jnp.sum(mine, axis=0, keepdims=True))
    inl_ids, xl_ids, cls_ids, live = lines

    seen = jnp.max(nav_rows[:n_inl, :], axis=0, keepdims=True)[:, OVER_LANE : OVER_LANE + 1]
    flag_send[...] = jnp.broadcast_to(seen, (BLOCK_TR, LANES))
    flag_recv[0] = flag_send[...]
    for step in range(1, n_xl):
        other = lax.rem(band + step, n_xl)
        push(flag_send, flag_recv.at[step], (flag_sems.at[0, step], flag_sems.at[1, step]), {"xl": other})

    weights = jnp.zeros((TAPS, depth), jnp.float32)
    for phase in range(PHASES):
        weights = jnp.where(cls_ids == float(phase), taps_ref[:, phase : phase + 1], weights)
    weights = weights * live
    tap_of = lax.broadcasted_iota(jnp.int32, (padded, depth), 0).astype(jnp.float32) - (xl_ids + 5.0)
    spread = jnp.zeros((padded, depth), jnp.float32)
    for tap in range(TAPS):
        spread = jnp.where(tap_of == float(tap), weights[tap : tap + 1], spread)

    def line(i, carry):
        rows = jnp.where(inl_ids == i.astype(jnp.float32), spread, 0.0)
        sums = jnp.broadcast_to(jnp.sum(rows, axis=1, keepdims=True), (padded, LANES))
        base = pl.multiple_of(i * width, width)
        inner[pl.ds(base, width), :] = rows[TAPS : TAPS + width].astype(jnp.bfloat16)
        fold_in[pl.ds(base, width), :] = sums[TAPS : TAPS + width]
        edge = pl.multiple_of(i * TAPS, TAPS)
        outer_f32[0, pl.ds(edge, TAPS), :] = rows[:TAPS]
        outer_f32[1, pl.ds(edge, TAPS), :] = rows[TAPS + width :]
        fold_send[0, pl.ds(edge, TAPS), :] = sums[:TAPS]
        fold_send[1, pl.ds(edge, TAPS), :] = sums[TAPS + width :]
        return carry

    lax.fori_loop(0, IL_DEV, line, 0)
    outer[...] = outer_f32[...].astype(jnp.bfloat16).reshape(2 * side, depth)

    for way, neighbour in ((0, left), (1, right)):
        push(
            fold_send.at[way],
            fold_recv.at[way],
            (fold_sems.at[0, way], fold_sems.at[1, way]),
            {"xl": neighbour},
        )

    from_right = jnp.where(band < n_xl - 1, 1.0, 0.0)
    from_left = jnp.where(band > 0, 1.0, 0.0)

    spread_second(2)
    push_first(3)

    for way in range(2):
        wait_for(fold_recv.at[way], fold_sems.at[1, way])

    def join(i, carry):
        edge = pl.multiple_of(i * TAPS, TAPS)
        first = pl.multiple_of(i * width, TAPS)
        last = pl.multiple_of(i * width + width - TAPS, TAPS)
        fold_in[pl.ds(last, TAPS), :] += fold_recv[0, pl.ds(edge, TAPS), :] * from_right
        fold_in[pl.ds(first, TAPS), :] += fold_recv[1, pl.ds(edge, TAPS), :] * from_left
        return carry

    lax.fori_loop(0, IL_DEV, join, 0)
    fold_in[...] = 1.0 / jnp.maximum(fold_in[...], 0.25)

    for step in range(1, n_xl):
        wait_for(flag_recv.at[step], flag_sems.at[1, step])
    flag_ref[...] = jnp.max(flag_recv[...], axis=0)

    def stage(c):
        lo, hi = span_of(c, length)
        size = hi - lo
        wait_for(y_recv.at[pl.ds(0, plane - 1), :, span(c)], y_sems.at[1, c])
        samples_in[half:, :size] = y_recv[:, :, lo:hi].reshape(half, size).astype(jnp.bfloat16)
        wait_for(p_recv.at[pl.ds(0, n_inl - 1), :, span(c)], p_sems.at[1, c])
        samples_in[:half, :size] = p_recv[:, :, lo:hi].reshape(half, size).astype(jnp.bfloat16)
        halo_send[:, :, lo:hi] = jnp.dot(
            outer[...], samples_in[:, :size], preferred_element_type=jnp.float32
        ).reshape(2, side, size)
        for way, neighbour in ((0, left), (1, right)):
            push(
                halo_send.at[way, :, span(c)],
                halo_recv.at[way, :, span(c)],
                (halo_sems.at[0, c, way], halo_sems.at[1, c, way]),
                {"xl": neighbour},
            )
        stack[:, lo:hi] = jnp.dot(
            inner[...], samples_in[:, :size], preferred_element_type=jnp.float32
        )

    def finish(c):
        lo, hi = span_of(c, length)
        for way in range(2):
            wait_for(halo_recv.at[way, :, span(c)], halo_sems.at[1, c, way])
        tile = 2 * width

        def body(m, carry):
            base = pl.multiple_of(m * tile, tile)
            for i in range(2):
                edge = pl.multiple_of(m * 2 * TAPS + i * TAPS, TAPS)
                first = pl.multiple_of(base + i * width, TAPS)
                last = pl.multiple_of(base + i * width + width - TAPS, TAPS)
                stack[pl.ds(last, TAPS), lo:hi] += halo_recv[0, pl.ds(edge, TAPS), lo:hi] * from_right
                stack[pl.ds(first, TAPS), lo:hi] += halo_recv[1, pl.ds(edge, TAPS), lo:hi] * from_left
            scale = fold_in[pl.ds(base, tile), 0:1]
            binned = (stack[pl.ds(base, tile), lo:hi] * scale).astype(jnp.bfloat16)
            if c == PARTS - 1:
                binned_ref[pl.ds(base, tile), :] = binned
                return carry
            part = jnp.dot(binned, resample[lo:hi, :], preferred_element_type=jnp.float32)
            if c > 0:
                part = part + total[pl.ds(base, tile), :]
            total[pl.ds(base, tile), :] = part
            return carry

        lax.fori_loop(0, IL_DEV // 2, body, 0)

    stage(0)
    finish(0)
    stage(1)
    spread_second(3)
    finish(1)
    stage(2)
    stage(3)
    finish(2)
    finish(3)

    wait_for(p_nav_send.at[pl.ds(0, n_inl - 1)], nav_sems.at[0, 0])
    wait_for(z_nav_send.at[pl.ds(0, layers - 1)], nav_sems.at[0, 1])
    wait_for(y_nav_send.at[pl.ds(0, plane - 1)], nav_sems.at[0, 2])
    for c in range(PARTS):
        wait_for(p_send.at[pl.ds(0, n_inl - 1), :, span(c)], p_sems.at[0, c])
        wait_for(z_send.at[pl.ds(0, layers - 1), :, span(c)], z_sems.at[0, c])
        wait_for(y_send.at[pl.ds(0, plane - 1), :, span(c)], y_sems.at[0, c])
        for way in range(2):
            wait_for(halo_send.at[way, :, span(c)], halo_sems.at[0, c, way])
    for way in range(2):
        wait_for(fold_send.at[way], fold_sems.at[0, way])
    for step in range(1, n_xl):
        wait_for(flag_send, flag_sems.at[0, step])


def finish_kernel(total_ref, binned_ref, tail_ref, out_hbm, rows, sem):
    tile = rows.shape[0] // 8

    def body(m, carry):
        base = pl.multiple_of(m * tile, tile)
        part = jnp.dot(
            binned_ref[pl.ds(base, tile), :], tail_ref[...], preferred_element_type=jnp.float32
        )
        rows[pl.ds(base, tile), :] = (total_ref[pl.ds(base, tile), :] + part).astype(jnp.bfloat16)
        pltpu.make_async_copy(
            rows.at[pl.ds(base, tile)], out_hbm.at[pl.ds(base, tile)], sem
        ).start()
        return carry

    lax.fori_loop(0, 8, body, 0)
    wait_for(rows, sem)


def pass_kernel(in_ref, out_ref):
    out_ref[...] = in_ref[...]


def per_device(traces, owner, counts, inline_off, xline_off, phase_cls):
    n_inl, n_xl = lax.axis_size("inl"), lax.axis_size("xl")
    plane = plane_of(n_inl)
    layers = n_inl // plane
    local_blocks, _, samples = traces.shape
    width = XLINES // n_xl
    large = widest(samples)
    last = span_of(PARTS - 1, samples)[1] - span_of(PARTS - 1, samples)[0]
    half = n_inl * BLOCK_TR
    side = IL_DEV * TAPS
    rows = IL_DEV * width
    in_vmem = pl.BlockSpec(memory_space=pltpu.VMEM)
    in_smem = pl.BlockSpec(memory_space=pltpu.SMEM)
    anywhere = pl.BlockSpec(memory_space=pl.ANY)
    table, nav, taps = pl.pallas_call(
        functools.partial(plan_kernel, n_inl),
        out_shape=(
            jax.ShapeDtypeStruct((n_inl + 8, LANES), jnp.int32),
            jax.ShapeDtypeStruct((local_blocks + 1, 1, LANES), jnp.float32),
            jax.ShapeDtypeStruct((TAPS, LANES), jnp.float32),
        ),
        in_specs=[in_vmem] * 5,
        out_specs=(in_vmem, in_vmem, in_vmem),
        compiler_params=pltpu.CompilerParams(vmem_limit_bytes=8 << 20),
    )(
        owner.reshape(1, local_blocks),
        counts.reshape(1, local_blocks),
        inline_off.T,
        xline_off.T,
        phase_cls.T,
    )
    f32, bf16 = jnp.float32, jnp.bfloat16
    scratch = [
        pltpu.VMEM((local_blocks, BLOCK_TR, samples), f32),
        pltpu.VMEM((n_inl, BLOCK_TR, samples), f32),
        pltpu.VMEM((n_inl, BLOCK_TR, samples), f32),
        pltpu.VMEM((layers, CAP * BLOCK_TR, samples), f32),
        pltpu.VMEM((layers, CAP * BLOCK_TR, samples), f32),
        pltpu.VMEM((plane, layers * BLOCK_TR, samples), f32),
        pltpu.VMEM((plane, layers * BLOCK_TR, samples), f32),
        pltpu.VMEM((n_inl, 1, LANES), f32),
        pltpu.VMEM((n_inl, 1, LANES), f32),
        pltpu.VMEM((layers, CAP, 1, LANES), f32),
        pltpu.VMEM((layers, CAP, 1, LANES), f32),
        pltpu.VMEM((plane, layers, 1, LANES), f32),
        pltpu.VMEM((plane, layers, 1, LANES), f32),
        pltpu.VMEM((layers, CAP, BLOCK_TR, LANES), f32),
        pltpu.VMEM((2 * n_inl, LANES), f32),
        pltpu.VMEM((2 * half, large), bf16),
        pltpu.VMEM((rows, 2 * half), bf16),
        pltpu.VMEM((2, side, 2 * half), f32),
        pltpu.VMEM((2 * side, 2 * half), bf16),
        pltpu.VMEM((samples, 2 * samples), bf16),
        pltpu.VMEM((rows, samples), f32),
        pltpu.VMEM((2, side, samples), f32),
        pltpu.VMEM((2, side, samples), f32),
        pltpu.VMEM((rows, LANES), f32),
        pltpu.VMEM((2, side, LANES), f32),
        pltpu.VMEM((2, side, LANES), f32),
        pltpu.VMEM((BLOCK_TR, LANES), f32),
        pltpu.VMEM((n_xl, BLOCK_TR, LANES), f32),
        pltpu.SemaphoreType.DMA,
        pltpu.SemaphoreType.DMA((2, PARTS)),
        pltpu.SemaphoreType.DMA((2, PARTS)),
        pltpu.SemaphoreType.DMA((2, PARTS)),
        pltpu.SemaphoreType.DMA((2, 3)),
        pltpu.SemaphoreType.DMA((2, PARTS, 2)),
        pltpu.SemaphoreType.DMA((2, 2)),
        pltpu.SemaphoreType.DMA((2, n_xl)),
    ]
    total, tail, binned, flag = pl.pallas_call(
        functools.partial(fast_kernel, n_inl, n_xl),
        out_shape=(
            jax.ShapeDtypeStruct((rows, 2 * samples), f32),
            jax.ShapeDtypeStruct((last, 2 * samples), bf16),
            jax.ShapeDtypeStruct((rows, last), bf16),
            jax.ShapeDtypeStruct((BLOCK_TR, LANES), f32),
        ),
        in_specs=[in_smem, anywhere, in_vmem, in_vmem],
        out_specs=(in_vmem, in_vmem, in_vmem, in_vmem),
        scratch_shapes=scratch,
        compiler_params=pltpu.CompilerParams(
            collective_id=0, has_side_effects=True, vmem_limit_bytes=36 << 20
        ),
    )(table, traces, nav, taps)

    def finish_fast():
        out = pl.pallas_call(
            finish_kernel,
            out_shape=jax.ShapeDtypeStruct((rows, 2 * samples), bf16),
            in_specs=[in_vmem] * 3,
            out_specs=pl.BlockSpec(memory_space=pltpu.HBM),
            scratch_shapes=[pltpu.VMEM((rows, 2 * samples), bf16), pltpu.SemaphoreType.DMA],
            compiler_params=pltpu.CompilerParams(vmem_limit_bytes=53 << 20),
        )(total, binned, tail)
        return out.reshape(IL_DEV, width, 2 * samples)

    def run_padded():
        out = padded_plan(traces, owner, counts, inline_off, xline_off, phase_cls)
        spec = pl.BlockSpec((2, width, 2 * samples), lambda m: (m, 0, 0))
        return pl.pallas_call(
            pass_kernel,
            grid=(IL_DEV // 2,),
            out_shape=jax.ShapeDtypeStruct(out.shape, out.dtype),
            in_specs=[spec],
            out_specs=spec,
            compiler_params=pltpu.CompilerParams(vmem_limit_bytes=12 << 20),
        )(out)

    return lax.cond(flag[0, 0] > 0.5, run_padded, finish_fast)


def solution(mesh):
    return jax.shard_map(
        per_device,
        mesh=mesh,
        in_specs=(
            P(("inl", "xl"), None, None),
            P(("inl", "xl"), None),
            P(("inl", "xl")),
            P(("inl", "xl"), None),
            P(("inl", "xl"), None),
            P(("inl", "xl"), None),
        ),
        out_specs=P("inl", "xl", None),
        check_vma=False,
    )
```

```python
import functools
import math

import jax
import jax.numpy as jnp
from jax import lax
from jax.experimental import pallas as pl
from jax.experimental.pallas import tpu as pltpu
from jax.sharding import PartitionSpec as P

XLINES = 256
TAPS = 8
PHASES = 16
BLOCK_TR = 8
SLOTS = 2
IL_DEV = 16
CHUNKS = 4
CAP = 3
LANES = 128
ROWS = SLOTS * BLOCK_TR
MESH = pl.DeviceIdType.MESH


def sinc_table():
    phase_idx = jnp.arange(PHASES, dtype=jnp.int32).astype(jnp.float32)[:, None]
    tap_idx = jnp.arange(TAPS, dtype=jnp.int32).astype(jnp.float32)[None, :]
    offset = tap_idx - 3.0 - phase_idx / PHASES
    return jnp.sinc(offset) * (0.5 + 0.5 * jnp.cos(math.pi * offset / 4.0))


def wait_for(ref, sem):
    pltpu.make_async_copy(ref, ref, sem).wait()


def build_resample(table_ref):
    length, width = table_ref.shape
    step = 16

    def body(part, carry):
        base = pl.multiple_of(part * step, step)
        rows_idx = lax.broadcasted_iota(jnp.int32, (step, width), 0) + base
        cols_idx = lax.broadcasted_iota(jnp.int32, (step, width), 1)
        lagged = (cols_idx >> 1) - rows_idx
        sign_val = (1 - 2 * (lagged & 1)).astype(jnp.float32)
        odd_val = sign_val / (math.pi * (lagged.astype(jnp.float32) + 0.5))
        even_val = (lagged == 0).astype(jnp.float32)
        table_ref[pl.ds(base, step), :] = jnp.where((cols_idx & 1) == 1, odd_val, even_val).astype(
            jnp.bfloat16
        )
        return carry

    lax.fori_loop(0, length // step, body, 0)


def padded_kernel(
    n_inl,
    n_xl,
    index_ref,
    traces_hbm,
    nav_ref,
    taps_ref,
    out_hbm,
    traces,
    send,
    recv,
    nav_send,
    nav_recv,
    inner,
    outer_f32,
    outer,
    resample,
    total,
    stack,
    out_rows,
    halo_send,
    halo_recv,
    fold_in,
    fold_send,
    fold_recv,
    load_sem,
    send_sems,
    recv_sems,
    nav_send_sem,
    nav_recv_sem,
    halo_send_sems,
    halo_recv_sems,
    fold_send_sems,
    fold_recv_sems,
    out_sem,
):
    me = lax.axis_index("inl")
    band = lax.axis_index("xl")
    right, left = lax.rem(band + 1, n_xl), lax.rem(band + n_xl - 1, n_xl)
    chunk = traces.shape[2] // CHUNKS
    depth = n_inl * ROWS
    width = inner.shape[0] // IL_DEV
    padded = width + 2 * TAPS
    side = IL_DEV * TAPS

    load = pltpu.make_async_copy(traces_hbm, traces, load_sem)
    load.start()

    barrier = pltpu.get_barrier_semaphore()

    def greet(off, carry):
        dest = lax.rem(me + off, n_inl)
        pl.semaphore_signal(barrier, inc=1, device_id={"inl": dest}, device_id_type=MESH)
        return carry

    lax.fori_loop(1, n_inl, greet, 0)
    for neighbour in (left, right):
        pl.semaphore_signal(barrier, inc=1, device_id={"xl": neighbour}, device_id_type=MESH)

    def gather_nav(off, carry):
        dest = lax.rem(me + off, n_inl)
        for slot in range(SLOTS):
            block = index_ref[dest, slot]
            nav_send[dest, slot * BLOCK_TR : (slot + 1) * BLOCK_TR, :] = nav_ref[block]
        return carry

    lax.fori_loop(0, n_inl, gather_nav, 0)
    nav_recv[me] = nav_send[me]
    load.wait()

    def gather(c):
        def body(off, carry):
            dest = lax.rem(me + off, n_inl)
            for slot in range(SLOTS):
                block = index_ref[dest, SLOTS + slot]
                send[c, dest, slot * BLOCK_TR : (slot + 1) * BLOCK_TR, :] = traces[
                    block, :, c * chunk : (c + 1) * chunk
                ]
            return carry

        lax.fori_loop(0, n_inl, body, 0)
        recv[c, me] = send[c, me]

    gather(0)
    pl.semaphore_wait(barrier, n_inl - 1 + 2)

    def push_nav(off, carry):
        dest = lax.rem(me + off, n_inl)
        pltpu.make_async_remote_copy(
            src_ref=nav_send.at[dest],
            dst_ref=nav_recv.at[me],
            send_sem=nav_send_sem,
            recv_sem=nav_recv_sem,
            device_id={"inl": dest},
            device_id_type=MESH,
        ).start()
        return carry

    lax.fori_loop(1, n_inl, push_nav, 0)

    def push(c):
        def body(off, carry):
            dest = lax.rem(me + off, n_inl)
            pltpu.make_async_remote_copy(
                src_ref=send.at[c, dest],
                dst_ref=recv.at[c, me],
                send_sem=send_sems.at[c],
                recv_sem=recv_sems.at[c],
                device_id={"inl": dest},
                device_id_type=MESH,
            ).start()
            return carry

        lax.fori_loop(1, n_inl, body, 0)

    for c in range(CHUNKS):
        if c + 1 < CHUNKS:
            gather(c + 1)
        push(c)

    build_resample(resample)

    wait_for(nav_recv.at[pl.ds(0, n_inl - 1)], nav_recv_sem)
    nav = nav_recv[...].reshape(depth, LANES).T
    inl_ids, xl_ids, cls_ids, live = nav[0:1], nav[1:2], nav[2:3], nav[3:4]
    weights = jnp.zeros((TAPS, depth), jnp.float32)
    for phase in range(PHASES):
        weights = jnp.where(cls_ids == float(phase), taps_ref[:, phase : phase + 1], weights)
    weights = weights * live
    tap_of = lax.broadcasted_iota(jnp.int32, (padded, depth), 0).astype(jnp.float32) - (xl_ids + 5.0)
    spread = jnp.zeros((padded, depth), jnp.float32)
    for tap in range(TAPS):
        spread = jnp.where(tap_of == float(tap), weights[tap : tap + 1], spread)

    def line(i, carry):
        rows = jnp.where(inl_ids == i.astype(jnp.float32), spread, 0.0)
        sums = jnp.broadcast_to(jnp.sum(rows, axis=1, keepdims=True), (padded, LANES))
        base = pl.multiple_of(i * width, width)
        inner[pl.ds(base, width), :] = rows[TAPS : TAPS + width].astype(jnp.bfloat16)
        fold_in[pl.ds(base, width), :] = sums[TAPS : TAPS + width]
        edge = pl.multiple_of(i * TAPS, TAPS)
        outer_f32[0, pl.ds(edge, TAPS), :] = rows[:TAPS]
        outer_f32[1, pl.ds(edge, TAPS), :] = rows[TAPS + width :]
        fold_send[0, pl.ds(edge, TAPS), :] = sums[:TAPS]
        fold_send[1, pl.ds(edge, TAPS), :] = sums[TAPS + width :]
        return carry

    lax.fori_loop(0, IL_DEV, line, 0)
    outer[...] = outer_f32[...].astype(jnp.bfloat16).reshape(2 * side, depth)

    folds = []
    for way, neighbour in ((0, left), (1, right)):
        copy = pltpu.make_async_remote_copy(
            src_ref=fold_send.at[way],
            dst_ref=fold_recv.at[way],
            send_sem=fold_send_sems.at[way],
            recv_sem=fold_recv_sems.at[way],
            device_id={"xl": neighbour},
            device_id_type=MESH,
        )
        copy.start()
        folds.append(copy)

    from_right = jnp.where(band < n_xl - 1, 1.0, 0.0)
    from_left = jnp.where(band > 0, 1.0, 0.0)

    for copy in folds:
        copy.wait()

    def join(i, carry):
        edge = pl.multiple_of(i * TAPS, TAPS)
        first = pl.multiple_of(i * width, TAPS)
        last = pl.multiple_of(i * width + width - TAPS, TAPS)
        fold_in[pl.ds(last, TAPS), :] += fold_recv[0, pl.ds(edge, TAPS), :] * from_right
        fold_in[pl.ds(first, TAPS), :] += fold_recv[1, pl.ds(edge, TAPS), :] * from_left
        return carry

    lax.fori_loop(0, IL_DEV, join, 0)
    fold_in[...] = 1.0 / jnp.maximum(fold_in[...], 0.25)

    halos = []
    for c in range(CHUNKS):
        wait_for(recv.at[c, pl.ds(0, n_inl - 1)], recv_sems.at[c])
        block = recv[c].reshape(depth, chunk).astype(jnp.bfloat16)
        halo_send[c] = jnp.dot(outer[...], block, preferred_element_type=jnp.float32).reshape(
            2, side, chunk
        )
        stack[...] = jnp.dot(inner[...], block, preferred_element_type=jnp.float32)
        sent = []
        for way, neighbour in ((0, left), (1, right)):
            copy = pltpu.make_async_remote_copy(
                src_ref=halo_send.at[c, way],
                dst_ref=halo_recv.at[c, way],
                send_sem=halo_send_sems.at[c, way],
                recv_sem=halo_recv_sems.at[c, way],
                device_id={"xl": neighbour},
                device_id_type=MESH,
            )
            copy.start()
            sent.append(copy)
        for copy in sent:
            copy.wait()

        def add_halo(i, carry, c=c):
            edge = pl.multiple_of(i * TAPS, TAPS)
            first = pl.multiple_of(i * width, TAPS)
            last = pl.multiple_of(i * width + width - TAPS, TAPS)
            stack[pl.ds(last, TAPS), :] += halo_recv[c, 0, pl.ds(edge, TAPS), :] * from_right
            stack[pl.ds(first, TAPS), :] += halo_recv[c, 1, pl.ds(edge, TAPS), :] * from_left
            return carry

        lax.fori_loop(0, IL_DEV, add_halo, 0)

        tile = out_rows.shape[0] // TAPS

        def finish(m, carry, c=c):
            base = pl.multiple_of(m * tile, tile)
            scale = fold_in[pl.ds(base, tile), 0:1]
            binned = (stack[pl.ds(base, tile), :] * scale).astype(jnp.bfloat16)
            part = jnp.dot(
                binned, resample[c * chunk : (c + 1) * chunk, :], preferred_element_type=jnp.float32
            )
            if c > 0:
                part = part + total[pl.ds(base, tile), :]
            if c < CHUNKS - 1:
                total[pl.ds(base, tile), :] = part
            else:
                out_rows[pl.ds(base, tile), :] = part.astype(jnp.bfloat16)
                pltpu.make_async_copy(
                    out_rows.at[pl.ds(base, tile)], out_hbm.at[pl.ds(base, tile)], out_sem
                ).start()
            return carry

        lax.fori_loop(0, TAPS, finish, 0)

    wait_for(nav_send.at[pl.ds(0, n_inl - 1)], nav_send_sem)
    for c in range(CHUNKS):
        wait_for(send.at[c, pl.ds(0, n_inl - 1)], send_sems.at[c])
    wait_for(out_rows, out_sem)


def padded_plan(traces, owner, counts, inline_off, xline_off, phase_cls):
    n_inl, n_xl = lax.axis_size("inl"), lax.axis_size("xl")
    local_blocks, _, samples = traces.shape
    width = XLINES // n_xl
    chunk = samples // CHUNKS
    depth = n_inl * ROWS
    side = IL_DEV * TAPS
    block_idx = jnp.arange(local_blocks, dtype=jnp.int32)
    named = owner[:, 0][None, :] == jnp.arange(n_inl, dtype=jnp.int32)[:, None]
    low = jnp.min(jnp.where(named, block_idx[None, :], local_blocks), axis=1)
    high = jnp.max(jnp.where(named, block_idx[None, :], -1), axis=1)
    high = jnp.where(high > low, high, local_blocks)
    nav_index = jnp.stack([low, high], axis=1)
    index = jnp.concatenate([nav_index, jnp.minimum(nav_index, local_blocks - 1)], axis=1)
    live = (jnp.arange(BLOCK_TR, dtype=jnp.int32)[None, :] < counts[:, None]).astype(jnp.float32)
    parts = [inline_off.astype(jnp.float32), xline_off.astype(jnp.float32)]
    parts = parts + [phase_cls.astype(jnp.float32), live]
    nav = jnp.stack(parts, axis=2)
    nav = jnp.pad(nav, ((0, 1), (0, 0), (0, LANES - len(parts))))
    taps = sinc_table().T
    scratch = [
        pltpu.VMEM((local_blocks, BLOCK_TR, samples), jnp.float32),
        pltpu.VMEM((CHUNKS, n_inl, ROWS, chunk), jnp.float32),
        pltpu.VMEM((CHUNKS, n_inl, ROWS, chunk), jnp.float32),
        pltpu.VMEM((n_inl, ROWS, LANES), jnp.float32),
        pltpu.VMEM((n_inl, ROWS, LANES), jnp.float32),
        pltpu.VMEM((IL_DEV * width, depth), jnp.bfloat16),
        pltpu.VMEM((2, side, depth), jnp.float32),
        pltpu.VMEM((2 * side, depth), jnp.bfloat16),
        pltpu.VMEM((samples, 2 * samples), jnp.bfloat16),
        pltpu.VMEM((IL_DEV * width, 2 * samples), jnp.float32),
        pltpu.VMEM((IL_DEV * width, chunk), jnp.float32),
        pltpu.VMEM((IL_DEV * width, 2 * samples), jnp.bfloat16),
        pltpu.VMEM((CHUNKS, 2, side, chunk), jnp.float32),
        pltpu.VMEM((CHUNKS, 2, side, chunk), jnp.float32),
        pltpu.VMEM((IL_DEV * width, LANES), jnp.float32),
        pltpu.VMEM((2, side, LANES), jnp.float32),
        pltpu.VMEM((2, side, LANES), jnp.float32),
        pltpu.SemaphoreType.DMA,
        pltpu.SemaphoreType.DMA((CHUNKS,)),
        pltpu.SemaphoreType.DMA((CHUNKS,)),
        pltpu.SemaphoreType.DMA,
        pltpu.SemaphoreType.DMA,
        pltpu.SemaphoreType.DMA((CHUNKS, 2)),
        pltpu.SemaphoreType.DMA((CHUNKS, 2)),
        pltpu.SemaphoreType.DMA((2,)),
        pltpu.SemaphoreType.DMA((2,)),
        pltpu.SemaphoreType.DMA,
    ]
    out = pl.pallas_call(
        functools.partial(padded_kernel, n_inl, n_xl),
        out_shape=jax.ShapeDtypeStruct((IL_DEV * width, 2 * samples), jnp.bfloat16),
        in_specs=[
            pl.BlockSpec(memory_space=pltpu.SMEM),
            pl.BlockSpec(memory_space=pl.ANY),
            pl.BlockSpec(memory_space=pltpu.VMEM),
            pl.BlockSpec(memory_space=pltpu.VMEM),
        ],
        out_specs=pl.BlockSpec(memory_space=pl.ANY),
        scratch_shapes=scratch,
        compiler_params=pltpu.CompilerParams(
            collective_id=1, has_side_effects=True, vmem_limit_bytes=44 << 20
        ),
    )(index, traces, nav, taps)
    return out.reshape(IL_DEV, width, 2 * samples)


OWN_LANE = 4 * BLOCK_TR
OVER_LANE = OWN_LANE + 1
EDGES = (0, 3, 5, 7, 8)
PARTS = len(EDGES) - 1


def span_of(c, length):
    return EDGES[c] * length // EDGES[-1], EDGES[c + 1] * length // EDGES[-1]


def widest(length):
    return max(hi - lo for lo, hi in [span_of(c, length) for c in range(PARTS)])


def plane_of(n_inl):
    return 8 if n_inl % 8 == 0 and n_inl > 8 else 2


def make_plan(n_inl, owner_ref, counts_ref, inl_ref, xl_ref, cls_ref, table_ref, nav_ref, taps_ref):
    blocks = owner_ref.shape[1]
    plane = plane_of(n_inl)
    named = owner_ref[...] == lax.broadcasted_iota(jnp.int32, (n_inl, blocks), 0)
    block_idx = lax.broadcasted_iota(jnp.int32, (n_inl, blocks), 1).astype(jnp.float32)
    low = jnp.min(jnp.where(named, block_idx, float(blocks)), axis=1, keepdims=True)
    high = jnp.max(jnp.where(named, block_idx, -1.0), axis=1, keepdims=True)
    two = jnp.broadcast_to(jnp.where(high > low, 1.0, 0.0), (n_inl, LANES))
    row_id = lax.broadcasted_iota(jnp.int32, (n_inl, n_inl), 0)
    col_id = lax.broadcasted_iota(jnp.int32, (n_inl, n_inl), 1)
    ahead = jnp.where((col_id < row_id) & (col_id // plane == row_id // plane), 1.0, 0.0)
    rank = jnp.dot(ahead, two, preferred_element_type=jnp.float32)
    own = lax.broadcasted_iota(jnp.int32, (n_inl, LANES), 0)
    lane = lax.broadcasted_iota(jnp.int32, (n_inl, LANES), 1)
    slot = (own // plane * CAP).astype(jnp.float32) + rank
    chosen = (two > 0.5) & (rank < CAP - 0.5) & (slot == lane.astype(jnp.float32))
    taken = jnp.sum(jnp.where(chosen, 1.0, 0.0), axis=0, keepdims=True)
    second = jnp.sum(jnp.where(chosen, high, 0.0), axis=0, keepdims=True)
    second = jnp.where(taken > 0.5, second, float(blocks))
    target = jnp.where(chosen, (own % plane + 1).astype(jnp.float32), 0.0)
    target = jnp.sum(target, axis=0, keepdims=True)
    over = jnp.where((two > 0.5) & (rank > CAP - 0.5), 1.0, 0.0)
    over = jnp.max(over, axis=0, keepdims=True)
    table_ref[:n_inl, :] = jnp.broadcast_to(low, (n_inl, LANES)).astype(jnp.int32)
    table_ref[n_inl : n_inl + 1, :] = second.astype(jnp.int32)
    table_ref[n_inl + 1 : n_inl + 2, :] = target.astype(jnp.int32)
    table_ref[n_inl + 2 : n_inl + 3, :] = over.astype(jnp.int32)
    table_ref[n_inl + 3 :, :] = jnp.zeros((5, LANES), jnp.int32)
    tap = lax.broadcasted_iota(jnp.int32, (TAPS, LANES), 0).astype(jnp.float32)
    offset = tap - 3.0 - lax.broadcasted_iota(jnp.int32, (TAPS, LANES), 1).astype(jnp.float32) / PHASES
    at_zero = offset == 0.0
    angle = math.pi * jnp.where(at_zero, 1.0, offset)
    sinc = jnp.where(at_zero, 1.0, jnp.sin(angle) / angle)
    taps_ref[...] = sinc * (0.5 + 0.5 * jnp.cos(math.pi * offset / 4.0))
    trace_idx = lax.broadcasted_iota(jnp.int32, (BLOCK_TR, blocks), 0)
    fields = [inl_ref[...], xl_ref[...], cls_ref[...], (trace_idx < counts_ref[...]).astype(jnp.int32)]
    fields = [field.astype(jnp.float32) for field in fields]
    unused = jnp.zeros((LANES - len(fields) * BLOCK_TR, blocks), jnp.float32)
    columns = jnp.concatenate(fields + [unused], axis=0)
    same_row = lax.broadcasted_iota(jnp.int32, (blocks, blocks), 0)
    same_col = lax.broadcasted_iota(jnp.int32, (blocks, blocks), 1)
    flat = lax.dot_general(
        jnp.where(same_row == same_col, 1.0, 0.0),
        columns,
        (((1,), (1,)), ((), ())),
        preferred_element_type=jnp.float32,
    )
    for block in range(blocks):
        nav_ref[block] = flat[block : block + 1]
    nav_ref[blocks] = jnp.zeros((1, LANES), jnp.float32)


def fast_kernel(
    n_inl,
    n_xl,
    owner_ref,
    counts_ref,
    inl_ref,
    xl_ref,
    cls_ref,
    traces_hbm,
    total,
    tail_ref,
    binned_ref,
    flag_ref,
    table_vmem,
    table_ref,
    nav_ref,
    taps_ref,
    traces,
    p_send,
    p_recv,
    z_send,
    z_recv,
    y_send,
    y_recv,
    p_nav_send,
    p_nav_recv,
    z_nav_send,
    z_nav_recv,
    y_nav_send,
    y_nav_recv,
    z_own,
    nav_rows,
    samples_in,
    inner,
    outer_f32,
    outer,
    resample,
    stack,
    halo_send,
    halo_recv,
    fold_in,
    fold_send,
    fold_recv,
    flag_send,
    flag_recv,
    load_sem,
    table_sem,
    p_sems,
    z_sems,
    y_sems,
    nav_sems,
    halo_sems,
    fold_sems,
    flag_sems,
):
    me = lax.axis_index("inl")
    band = lax.axis_index("xl")
    plane = plane_of(n_inl)
    layers = n_inl // plane
    layer, place = me // plane, lax.rem(me, plane)
    right, left = lax.rem(band + 1, n_xl), lax.rem(band + n_xl - 1, n_xl)
    length = traces.shape[2]
    blocks = traces.shape[0]
    half = n_inl * BLOCK_TR
    depth = 2 * half
    width = inner.shape[0] // IL_DEV
    padded = width + 2 * TAPS
    side = IL_DEV * TAPS

    load = pltpu.make_async_copy(traces_hbm, traces, load_sem)
    load.start()

    barrier = pltpu.get_barrier_semaphore()

    def greet(off, carry):
        dest = lax.rem(me + 1 + lax.rem(off + n_inl * 7 // 16, n_inl - 1), n_inl)
        pl.semaphore_signal(barrier, inc=1, device_id={"inl": dest}, device_id_type=MESH)
        return carry

    lax.fori_loop(0, n_inl - 1, greet, 0)
    for step in range(1, n_xl):
        other = lax.rem(band + step, n_xl)
        pl.semaphore_signal(barrier, inc=1, device_id={"xl": other}, device_id_type=MESH)

    field_id = lax.broadcasted_iota(jnp.int32, (1, LANES), 1)
    make_plan(n_inl, owner_ref, counts_ref, inl_ref, xl_ref, cls_ref, table_vmem, nav_ref, taps_ref)
    table = pltpu.make_async_copy(table_vmem, table_ref, table_sem)
    table.start()
    load.wait()
    table.wait()
    over = table_ref[n_inl + 2, 0].astype(jnp.float32)

    def gather_second(layer_to, carry):
        for r in range(CAP):
            spot = layer_to * CAP + r
            block = jnp.clip(table_ref[n_inl, spot], 0, blocks)
            target = table_ref[n_inl + 1, spot].astype(jnp.float32)
            z_nav_send[layer_to, r] = jnp.where(field_id == OWN_LANE, target, nav_ref[block])
            z_send[layer_to, r * BLOCK_TR : (r + 1) * BLOCK_TR, :] = traces[
                jnp.minimum(block, blocks - 1)
            ]
        return carry

    lax.fori_loop(0, layers, gather_second, 0)

    def gather_first(off, carry):
        dest = lax.rem(me + off, n_inl)
        block = jnp.clip(table_ref[dest, 0], 0, blocks)
        p_nav_send[dest] = jnp.where(field_id == OVER_LANE, over, nav_ref[block])
        p_send[dest] = traces[jnp.minimum(block, blocks - 1)]
        return carry

    lax.fori_loop(0, n_inl, gather_first, 0)
    p_nav_recv[me] = p_nav_send[me]
    p_recv[me] = p_send[me]
    z_nav_recv[layer] = z_nav_send[layer]
    z_recv[layer] = z_send[layer]

    pl.semaphore_wait(barrier, n_inl - 1 + n_xl - 1)

    def span(c):
        lo, hi = span_of(c, length)
        return pl.ds(lo, hi - lo)

    def away(off):
        reach = (off + 1) // 2
        return lax.rem(layer + jnp.where(lax.rem(off, 2) == 1, reach, layers - reach), layers)

    def partner(off):
        return away(lax.rem(off, layers)) * plane + lax.rem(place + off // layers, plane)

    def push(source, target, sems, to):
        pltpu.make_async_remote_copy(
            src_ref=source,
            dst_ref=target,
            send_sem=sems[0],
            recv_sem=sems[1],
            device_id=to,
            device_id_type=MESH,
        ).start()

    def push_first(c):
        def body(off, carry):
            dest = partner(off)
            push(
                p_send.at[dest, :, span(c)],
                p_recv.at[me, :, span(c)],
                (p_sems.at[0, c], p_sems.at[1, c]),
                {"inl": dest},
            )
            return carry

        lax.fori_loop(1, n_inl, body, 0)

    def push_second(c):
        def body(off, carry):
            to = away(off)
            push(
                z_send.at[to, :, span(c)],
                z_recv.at[layer, :, span(c)],
                (z_sems.at[0, c], z_sems.at[1, c]),
                {"inl": to * plane + place},
            )
            return carry

        lax.fori_loop(1, layers, body, 0)

    def spread_second(c):
        lo, hi = span_of(c, length)
        wait_for(z_recv.at[pl.ds(0, layers - 1), :, span(c)], z_sems.at[1, c])

        def body(to, carry):
            wanted = (to + 1).astype(jnp.float32)
            for origin in range(layers):
                held = jnp.zeros((BLOCK_TR, hi - lo), jnp.float32)
                for r in range(CAP):
                    named = z_own[origin, r, :, 0:1] == wanted
                    value = z_recv[origin, r * BLOCK_TR : (r + 1) * BLOCK_TR, lo:hi]
                    held = jnp.where(named, value, held)
                y_send[to, origin * BLOCK_TR : (origin + 1) * BLOCK_TR, lo:hi] = held
            return carry

        lax.fori_loop(0, plane, body, 0)
        y_recv[place, :, lo:hi] = y_send[place, :, lo:hi]

        def send(off, carry):
            to = lax.rem(place + off, plane)
            push(
                y_send.at[to, :, span(c)],
                y_recv.at[place, :, span(c)],
                (y_sems.at[0, c], y_sems.at[1, c]),
                {"inl": layer * plane + to},
            )
            return carry

        lax.fori_loop(1, plane, send, 0)

    def push_z_nav(off, carry):
        to = lax.rem(layer + off, layers)
        push(
            z_nav_send.at[to],
            z_nav_recv.at[layer],
            (nav_sems.at[0, 1], nav_sems.at[1, 1]),
            {"inl": to * plane + place},
        )
        return carry

    def push_p_nav(off, carry):
        dest = lax.rem(me + off, n_inl)
        push(
            p_nav_send.at[dest],
            p_nav_recv.at[me],
            (nav_sems.at[0, 0], nav_sems.at[1, 0]),
            {"inl": dest},
        )
        return carry

    push_second(0)
    lax.fori_loop(1, layers, push_z_nav, 0)
    push_second(1)
    push_first(0)
    lax.fori_loop(1, n_inl, push_p_nav, 0)
    push_second(2)
    push_first(1)

    wait_for(z_nav_recv.at[pl.ds(0, layers - 1)], nav_sems.at[1, 1])

    for origin in range(layers):
        for r in range(CAP):
            own = z_nav_recv[origin, r][:, OWN_LANE : OWN_LANE + 1]
            z_own[origin, r] = jnp.broadcast_to(own, (BLOCK_TR, LANES))

    def spread_nav(to, carry):
        wanted = (to + 1).astype(jnp.float32)
        for origin in range(layers):
            held = jnp.zeros((1, LANES), jnp.float32)
            for r in range(CAP):
                held = jnp.where(z_own[origin, r, 0:1, 0:1] == wanted, z_nav_recv[origin, r], held)
            y_nav_send[to, origin] = held
        return carry

    lax.fori_loop(0, plane, spread_nav, 0)
    y_nav_recv[place] = y_nav_send[place]

    def push_y_nav(off, carry):
        to = lax.rem(place + off, plane)
        push(
            y_nav_send.at[to],
            y_nav_recv.at[place],
            (nav_sems.at[0, 2], nav_sems.at[1, 2]),
            {"inl": layer * plane + to},
        )
        return carry

    lax.fori_loop(1, plane, push_y_nav, 0)
    spread_second(0)
    build_resample(resample)
    tail_ref[...] = resample[span_of(PARTS - 1, length)[0] :, :]
    spread_second(1)
    push_second(3)
    push_first(2)

    wait_for(p_nav_recv.at[pl.ds(0, n_inl - 1)], nav_sems.at[1, 0])
    wait_for(y_nav_recv.at[pl.ds(0, plane - 1)], nav_sems.at[1, 2])
    def first_row(row, carry):
        nav_rows[pl.ds(row, 1), :] = p_nav_recv[row]
        return carry

    lax.fori_loop(0, n_inl, first_row, 0)

    def second_row(origin, carry):
        for to in range(plane):
            nav_rows[pl.ds(n_inl + to * layers + origin, 1), :] = y_nav_recv[to, origin]
        return carry

    lax.fori_loop(0, layers, second_row, 0)
    column = lax.broadcasted_iota(jnp.int32, (LANES, depth), 1)
    source = lax.broadcasted_iota(jnp.int32, (LANES, depth), 0)
    owner_row = lax.broadcasted_iota(jnp.int32, (2 * n_inl, depth), 0)
    owner_col = lax.broadcasted_iota(jnp.int32, (2 * n_inl, depth), 1)
    lines = []
    for field in range(4):
        pick = jnp.where(source == field * BLOCK_TR + column % BLOCK_TR, 1.0, 0.0)
        wide = jnp.dot(nav_rows[...], pick, preferred_element_type=jnp.float32)
        mine = jnp.where(owner_row == owner_col // BLOCK_TR, wide, 0.0)
        lines.append(jnp.sum(mine, axis=0, keepdims=True))
    inl_ids, xl_ids, cls_ids, live = lines

    seen = jnp.max(nav_rows[:n_inl, :], axis=0, keepdims=True)[:, OVER_LANE : OVER_LANE + 1]
    flag_send[...] = jnp.broadcast_to(seen, (BLOCK_TR, LANES))
    flag_recv[0] = flag_send[...]
    for step in range(1, n_xl):
        other = lax.rem(band + step, n_xl)
        push(flag_send, flag_recv.at[step], (flag_sems.at[0, step], flag_sems.at[1, step]), {"xl": other})

    weights = jnp.zeros((TAPS, depth), jnp.float32)
    for phase in range(PHASES):
        weights = jnp.where(cls_ids == float(phase), taps_ref[:, phase : phase + 1], weights)
    weights = weights * live
    tap_of = lax.broadcasted_iota(jnp.int32, (padded, depth), 0).astype(jnp.float32) - (xl_ids + 5.0)
    spread = jnp.zeros((padded, depth), jnp.float32)
    for tap in range(TAPS):
        spread = jnp.where(tap_of == float(tap), weights[tap : tap + 1], spread)

    def line(i, carry):
        rows = jnp.where(inl_ids == i.astype(jnp.float32), spread, 0.0)
        sums = jnp.broadcast_to(jnp.sum(rows, axis=1, keepdims=True), (padded, LANES))
        base = pl.multiple_of(i * width, width)
        inner[pl.ds(base, width), :] = rows[TAPS : TAPS + width].astype(jnp.bfloat16)
        fold_in[pl.ds(base, width), :] = sums[TAPS : TAPS + width]
        edge = pl.multiple_of(i * TAPS, TAPS)
        outer_f32[0, pl.ds(edge, TAPS), :] = rows[:TAPS]
        outer_f32[1, pl.ds(edge, TAPS), :] = rows[TAPS + width :]
        fold_send[0, pl.ds(edge, TAPS), :] = sums[:TAPS]
        fold_send[1, pl.ds(edge, TAPS), :] = sums[TAPS + width :]
        return carry

    lax.fori_loop(0, IL_DEV, line, 0)
    outer[...] = outer_f32[...].astype(jnp.bfloat16).reshape(2 * side, depth)

    for way, neighbour in ((0, left), (1, right)):
        push(
            fold_send.at[way],
            fold_recv.at[way],
            (fold_sems.at[0, way], fold_sems.at[1, way]),
            {"xl": neighbour},
        )

    from_right = jnp.where(band < n_xl - 1, 1.0, 0.0)
    from_left = jnp.where(band > 0, 1.0, 0.0)

    spread_second(2)
    push_first(3)

    for way in range(2):
        wait_for(fold_recv.at[way], fold_sems.at[1, way])

    def join(i, carry):
        edge = pl.multiple_of(i * TAPS, TAPS)
        first = pl.multiple_of(i * width, TAPS)
        last = pl.multiple_of(i * width + width - TAPS, TAPS)
        fold_in[pl.ds(last, TAPS), :] += fold_recv[0, pl.ds(edge, TAPS), :] * from_right
        fold_in[pl.ds(first, TAPS), :] += fold_recv[1, pl.ds(edge, TAPS), :] * from_left
        return carry

    lax.fori_loop(0, IL_DEV, join, 0)
    fold_in[...] = 1.0 / jnp.maximum(fold_in[...], 0.25)

    for step in range(1, n_xl):
        wait_for(flag_recv.at[step], flag_sems.at[1, step])
    flag_ref[...] = jnp.max(flag_recv[...], axis=0)

    def stage(c):
        lo, hi = span_of(c, length)
        size = hi - lo
        wait_for(y_recv.at[pl.ds(0, plane - 1), :, span(c)], y_sems.at[1, c])
        samples_in[half:, :size] = y_recv[:, :, lo:hi].reshape(half, size).astype(jnp.bfloat16)
        wait_for(p_recv.at[pl.ds(0, n_inl - 1), :, span(c)], p_sems.at[1, c])
        samples_in[:half, :size] = p_recv[:, :, lo:hi].reshape(half, size).astype(jnp.bfloat16)
        halo_send[:, :, lo:hi] = jnp.dot(
            outer[...], samples_in[:, :size], preferred_element_type=jnp.float32
        ).reshape(2, side, size)
        for way, neighbour in ((0, left), (1, right)):
            push(
                halo_send.at[way, :, span(c)],
                halo_recv.at[way, :, span(c)],
                (halo_sems.at[0, c, way], halo_sems.at[1, c, way]),
                {"xl": neighbour},
            )
        stack[:, lo:hi] = jnp.dot(
            inner[...], samples_in[:, :size], preferred_element_type=jnp.float32
        )

    def finish(c):
        lo, hi = span_of(c, length)
        for way in range(2):
            wait_for(halo_recv.at[way, :, span(c)], halo_sems.at[1, c, way])
        tile = 2 * width

        def body(m, carry):
            base = pl.multiple_of(m * tile, tile)
            for i in range(2):
                edge = pl.multiple_of(m * 2 * TAPS + i * TAPS, TAPS)
                first = pl.multiple_of(base + i * width, TAPS)
                last = pl.multiple_of(base + i * width + width - TAPS, TAPS)
                stack[pl.ds(last, TAPS), lo:hi] += halo_recv[0, pl.ds(edge, TAPS), lo:hi] * from_right
                stack[pl.ds(first, TAPS), lo:hi] += halo_recv[1, pl.ds(edge, TAPS), lo:hi] * from_left
            scale = fold_in[pl.ds(base, tile), 0:1]
            binned = (stack[pl.ds(base, tile), lo:hi] * scale).astype(jnp.bfloat16)
            if c == PARTS - 1:
                binned_ref[pl.ds(base, tile), :] = binned
                return carry
            part = jnp.dot(binned, resample[lo:hi, :], preferred_element_type=jnp.float32)
            if c > 0:
                part = part + total[pl.ds(base, tile), :]
            total[pl.ds(base, tile), :] = part
            return carry

        lax.fori_loop(0, IL_DEV // 2, body, 0)

    stage(0)
    finish(0)
    stage(1)
    spread_second(3)
    finish(1)
    stage(2)
    stage(3)
    finish(2)
    finish(3)

    wait_for(p_nav_send.at[pl.ds(0, n_inl - 1)], nav_sems.at[0, 0])
    wait_for(z_nav_send.at[pl.ds(0, layers - 1)], nav_sems.at[0, 1])
    wait_for(y_nav_send.at[pl.ds(0, plane - 1)], nav_sems.at[0, 2])
    for c in range(PARTS):
        wait_for(p_send.at[pl.ds(0, n_inl - 1), :, span(c)], p_sems.at[0, c])
        wait_for(z_send.at[pl.ds(0, layers - 1), :, span(c)], z_sems.at[0, c])
        wait_for(y_send.at[pl.ds(0, plane - 1), :, span(c)], y_sems.at[0, c])
        for way in range(2):
            wait_for(halo_send.at[way, :, span(c)], halo_sems.at[0, c, way])
    for way in range(2):
        wait_for(fold_send.at[way], fold_sems.at[0, way])
    for step in range(1, n_xl):
        wait_for(flag_send, flag_sems.at[0, step])


def finish_kernel(total_ref, binned_ref, tail_ref, out_hbm, rows, sem):
    tile = rows.shape[0] // 8

    def body(m, carry):
        base = pl.multiple_of(m * tile, tile)
        part = jnp.dot(
            binned_ref[pl.ds(base, tile), :], tail_ref[...], preferred_element_type=jnp.float32
        )
        rows[pl.ds(base, tile), :] = (total_ref[pl.ds(base, tile), :] + part).astype(jnp.bfloat16)
        pltpu.make_async_copy(
            rows.at[pl.ds(base, tile)], out_hbm.at[pl.ds(base, tile)], sem
        ).start()
        return carry

    lax.fori_loop(0, 8, body, 0)
    wait_for(rows, sem)


def pass_kernel(in_ref, out_ref):
    out_ref[...] = in_ref[...]


def per_device(traces, owner, counts, inline_off, xline_off, phase_cls):
    n_inl, n_xl = lax.axis_size("inl"), lax.axis_size("xl")
    plane = plane_of(n_inl)
    layers = n_inl // plane
    local_blocks, _, samples = traces.shape
    width = XLINES // n_xl
    large = widest(samples)
    last = span_of(PARTS - 1, samples)[1] - span_of(PARTS - 1, samples)[0]
    half = n_inl * BLOCK_TR
    side = IL_DEV * TAPS
    rows = IL_DEV * width
    in_vmem = pl.BlockSpec(memory_space=pltpu.VMEM)
    anywhere = pl.BlockSpec(memory_space=pl.ANY)
    f32, bf16 = jnp.float32, jnp.bfloat16
    scratch = [
        pltpu.VMEM((n_inl + 8, LANES), jnp.int32),
        pltpu.SMEM((n_inl + 8, LANES), jnp.int32),
        pltpu.VMEM((local_blocks + 1, 1, LANES), f32),
        pltpu.VMEM((TAPS, LANES), f32),
        pltpu.VMEM((local_blocks, BLOCK_TR, samples), f32),
        pltpu.VMEM((n_inl, BLOCK_TR, samples), f32),
        pltpu.VMEM((n_inl, BLOCK_TR, samples), f32),
        pltpu.VMEM((layers, CAP * BLOCK_TR, samples), f32),
        pltpu.VMEM((layers, CAP * BLOCK_TR, samples), f32),
        pltpu.VMEM((plane, layers * BLOCK_TR, samples), f32),
        pltpu.VMEM((plane, layers * BLOCK_TR, samples), f32),
        pltpu.VMEM((n_inl, 1, LANES), f32),
        pltpu.VMEM((n_inl, 1, LANES), f32),
        pltpu.VMEM((layers, CAP, 1, LANES), f32),
        pltpu.VMEM((layers, CAP, 1, LANES), f32),
        pltpu.VMEM((plane, layers, 1, LANES), f32),
        pltpu.VMEM((plane, layers, 1, LANES), f32),
        pltpu.VMEM((layers, CAP, BLOCK_TR, LANES), f32),
        pltpu.VMEM((2 * n_inl, LANES), f32),
        pltpu.VMEM((2 * half, large), bf16),
        pltpu.VMEM((rows, 2 * half), bf16),
        pltpu.VMEM((2, side, 2 * half), f32),
        pltpu.VMEM((2 * side, 2 * half), bf16),
        pltpu.VMEM((samples, 2 * samples), bf16),
        pltpu.VMEM((rows, samples), f32),
        pltpu.VMEM((2, side, samples), f32),
        pltpu.VMEM((2, side, samples), f32),
        pltpu.VMEM((rows, LANES), f32),
        pltpu.VMEM((2, side, LANES), f32),
        pltpu.VMEM((2, side, LANES), f32),
        pltpu.VMEM((BLOCK_TR, LANES), f32),
        pltpu.VMEM((n_xl, BLOCK_TR, LANES), f32),
        pltpu.SemaphoreType.DMA,
        pltpu.SemaphoreType.DMA,
        pltpu.SemaphoreType.DMA((2, PARTS)),
        pltpu.SemaphoreType.DMA((2, PARTS)),
        pltpu.SemaphoreType.DMA((2, PARTS)),
        pltpu.SemaphoreType.DMA((2, 3)),
        pltpu.SemaphoreType.DMA((2, PARTS, 2)),
        pltpu.SemaphoreType.DMA((2, 2)),
        pltpu.SemaphoreType.DMA((2, n_xl)),
    ]
    total, tail, binned, flag = pl.pallas_call(
        functools.partial(fast_kernel, n_inl, n_xl),
        out_shape=(
            jax.ShapeDtypeStruct((rows, 2 * samples), f32),
            jax.ShapeDtypeStruct((last, 2 * samples), bf16),
            jax.ShapeDtypeStruct((rows, last), bf16),
            jax.ShapeDtypeStruct((BLOCK_TR, LANES), f32),
        ),
        in_specs=[in_vmem] * 5 + [anywhere],
        out_specs=(in_vmem, in_vmem, in_vmem, in_vmem),
        scratch_shapes=scratch,
        compiler_params=pltpu.CompilerParams(
            collective_id=0, has_side_effects=True, vmem_limit_bytes=36 << 20
        ),
    )(
        owner.reshape(1, local_blocks),
        counts.reshape(1, local_blocks),
        inline_off.T,
        xline_off.T,
        phase_cls.T,
        traces,
    )

    def finish_fast():
        out = pl.pallas_call(
            finish_kernel,
            out_shape=jax.ShapeDtypeStruct((rows, 2 * samples), bf16),
            in_specs=[in_vmem] * 3,
            out_specs=pl.BlockSpec(memory_space=pltpu.HBM),
            scratch_shapes=[pltpu.VMEM((rows, 2 * samples), bf16), pltpu.SemaphoreType.DMA],
            compiler_params=pltpu.CompilerParams(vmem_limit_bytes=53 << 20),
        )(total, binned, tail)
        return out.reshape(IL_DEV, width, 2 * samples)

    def run_padded():
        out = padded_plan(traces, owner, counts, inline_off, xline_off, phase_cls)
        spec = pl.BlockSpec((2, width, 2 * samples), lambda m: (m, 0, 0))
        return pl.pallas_call(
            pass_kernel,
            grid=(IL_DEV // 2,),
            out_shape=jax.ShapeDtypeStruct(out.shape, out.dtype),
            in_specs=[spec],
            out_specs=spec,
            compiler_params=pltpu.CompilerParams(vmem_limit_bytes=12 << 20),
        )(out)

    return lax.cond(flag[0, 0] > 0.5, run_padded, finish_fast)


def solution(mesh):
    return jax.shard_map(
        per_device,
        mesh=mesh,
        in_specs=(
            P(("inl", "xl"), None, None),
            P(("inl", "xl"), None),
            P(("inl", "xl")),
            P(("inl", "xl"), None),
            P(("inl", "xl"), None),
            P(("inl", "xl"), None),
        ),
        out_specs=P("inl", "xl", None),
        check_vma=False,
    )
```
